512 devices in a mesh: tok: 8 (over x, core), voc: 64 (over z, y).
Axes of the slice: x: 4, y: 4, z: 16, core: 2. Of those that a mesh axis runs over, the one named last changes fastest.
Arguments:
- teacher_hidden: bfloat16 [1024, 8192], P('voc', 'tok'), may hold values from -8 to 8
- teacher_head: bfloat16 [8192, 65536], P('tok', 'voc'), may hold values from -1 to 1
- student_hidden: bfloat16 [1024, 1536], P('tok'), may hold values from -8 to 8
- student_head: bfloat16 [1536, 81920], P('tok', 'voc'), may hold values from -1 to 1
- pair_owner: int32 [512, 8], replicated, may hold values from 0 to 63, all different within a row; in each aligned block of 8 rows (0 to 7, 8 to 15, ...) at most 2 rows name the same one
- pair_block: int32 [512, 8], replicated, may hold values from 0 to 9
- pair_shift: int32 [512, 8], replicated, may hold values from 0 to 127
- pair_count: int32 [512, 8], replicated, may hold values from 1 to 8
Outputs:
- token_loss: float32 [1024], P('tok')
- hidden_grad: bfloat16 [1024, 1536], P('tok')
The draws below stay inside these ranges and needn't reach their ends.
Inputs may be any that keep to these rules, and one draw needn't show every extreme that they name: `pair_owner`: each row names 8 different owners. Within the 8 rows of the teacher blocks of one index of voc (aligned blocks of 8 rows) no owner is named more than 2 times, and in every draw some owner is named exactly 2 times in some such block. Every owner is named somewhere.
All inputs are finite; a program needn't handle non-finite values.
Results may differ from the reference program's by a relative error of at most 0.0046.
Values may be sent and summed in bfloat16 or wider, within the bound.
No kernel may reach another device: no remote copies, remote signals or barrier semaphores. Data moves between devices by JAX's collectives and lax.ppermute only.
A program may use at most 64 MiB of HBM per device.

```python
import math
import jax
import jax.numpy as jnp
import numpy as np
from jax import lax

DT = 8192
DS = 1536
BLOCK = 128
TB_DEV = 8
SB_DEV = 10
FANOUT = 8
CAP = 2
TOKENS = 1024
TBLOCKS = 512
VT = 65536
VS = 81920
N_VOC = 64


def head_column(column_key, column, width):
    values = jax.random.normal(jax.random.fold_in(column_key, column), (width,), jnp.float32)
    values = jnp.clip(jnp.clip(values, -6.0, 6.0) * (3.0 / math.sqrt(width)), -1.0, 1.0)
    return values.astype(jnp.bfloat16).astype(jnp.float32)


def head_matrix(column_key, width, vocab):
    columns = jax.vmap(lambda column: head_column(column_key, column, width))(jnp.arange(vocab, dtype=jnp.int32))
    return columns.T


def hidden_rows(key, salt, rows, width):
    base_key = jax.random.fold_in(key, salt * 10 + 1)
    values = jnp.clip(jax.random.normal(base_key, (rows, width), jnp.float32), -6.0, 6.0)
    return jnp.clip(values, -8.0, 8.0)


def draw_teacher_hidden(key, part):
    return hidden_rows(key, 3, TOKENS, DT).astype(jnp.bfloat16)


def draw_teacher_head(key, part):
    return head_matrix(jax.random.fold_in(key, 11), DT, VT).astype(jnp.bfloat16)


def draw_student_hidden(key, part):
    return hidden_rows(key, 4, TOKENS, DS).astype(jnp.bfloat16)


def draw_student_head(key, part):
    return head_matrix(jax.random.fold_in(key, 12), DS, VS).astype(jnp.bfloat16)


def with_ends(drawn, key, least, high):
    longest = drawn.shape.index(max(drawn.shape))
    spots = []
    for shift in (0, 1):
        where = [jax.random.randint(jax.random.fold_in(key, axis), (), 0, length) for axis, length in enumerate(drawn.shape)]
        where[longest] = (where[longest] + shift) % drawn.shape[longest]
        spots.append(tuple(where))
    return drawn.at[spots[0]].set(least).at[spots[1]].set(high)


def deal_out(stream_key, own, number, rows, number_of, top, most, lean):
    order = jax.random.permutation(stream_key, number_of)
    heavy_load, usual = portions_of(number_of, rows * top, most, lean, True), portions_of(number_of, rows * top, most, lean, False)
    places = jnp.arange(number_of)

    def named(lengths, turn):
        used = int((lengths > 0).sum())
        fixed = max(1, used // 4)
        moved = fixed + (places - fixed + turn * (used - fixed)) % max(1, number_of - fixed)
        return jnp.zeros((number_of,), jnp.int32).at[order[jnp.where(places < fixed, places, moved)]].set(jnp.asarray(lengths, jnp.int32))

    lengths = jnp.where(number % 4 == 0, named(heavy_load, number // 4), named(usual, number - number // 4 - 1))
    mixed = jax.random.permutation(jax.random.fold_in(own, 3), number_of)
    source_of, taker = mixed[0:number_of // 2 * 2:2], mixed[1:number_of // 2 * 2:2]
    slack = jnp.minimum(lengths[source_of] - 1, most - lengths[taker]) // 2
    slack = jnp.where((source_of == order[0]) | (taker == order[0]) | (lengths[taker] == 0), 0, jnp.maximum(slack, 0))
    moved = jax.random.randint(jax.random.fold_in(own, 4), (number_of // 2,), 0, 1 << 20) % (slack + 1)
    lengths = lengths.at[source_of].add(-moved).at[taker].add(moved)
    members = jnp.searchsorted(jnp.cumsum(lengths), jnp.arange(rows * top), side="right").astype(jnp.int32)
    listing = members.reshape(top, rows).T
    listing = listing[jax.random.permutation(jax.random.fold_in(own, 1), rows)]
    turn = jax.random.randint(jax.random.fold_in(own, 2), (rows, 1), 0, top)
    return jnp.take_along_axis(listing, (jnp.arange(top)[None, :] + turn) % top, axis=1)


def portions_of(count, total, most, slope, full):
    weights = [(1 << 20) // math.isqrt(grade ** slope) + 1 for grade in range(1, count + 1)]
    largest = most if full else min(most, max(-(-total // count), total * weights[0] // sum(weights)))
    least = 1 if total - largest >= count - 1 else 0
    holding, rest = [largest] + [least] * (count - 1), total - largest - least * (count - 1)
    while rest > 0:
        free = [i for i in range(1, count) if holding[i] < largest] or [i for i in range(1, count) if holding[i] < most]
        mass, left = sum([weights[i] for i in free]), rest
        for i in free:
            more = min(most - holding[i], max(1, left * weights[i] // mass), rest)
            holding[i] = holding[i] + more
            rest = rest - more
    return np.array(holding)


def setup_inputs(seed: int = 0) -> dict:
    arg_keys = jax.random.split(jax.random.key(seed), 9)
    teacher_hidden = draw_teacher_hidden(jax.random.fold_in(arg_keys[8], 71), 0)
    teacher_head = draw_teacher_head(jax.random.fold_in(arg_keys[8], 71), 0)
    student_hidden = draw_student_hidden(jax.random.fold_in(arg_keys[8], 71), 0)
    student_head = draw_student_head(jax.random.fold_in(arg_keys[8], 71), 0)
    pair_owner_keys = jax.random.split(jax.random.fold_in(arg_keys[4], 1), TBLOCKS // TB_DEV)
    pair_owner_turns = jax.random.permutation(jax.random.fold_in(arg_keys[4], 3), TBLOCKS // TB_DEV)
    pair_owner = jax.vmap(lambda own, number: deal_out(jax.random.fold_in(arg_keys[4], 2), own, number, TB_DEV, N_VOC, FANOUT, CAP, 2))(pair_owner_keys, pair_owner_turns).reshape((TBLOCKS, FANOUT))
    pair_block = with_ends(jax.random.randint(arg_keys[5], (TBLOCKS, FANOUT), 0, SB_DEV), jax.random.fold_in(arg_keys[5], 1), 0, SB_DEV - 1).astype(jnp.int32)
    pair_shift = with_ends(jax.random.randint(arg_keys[6], (TBLOCKS, FANOUT), 0, BLOCK), jax.random.fold_in(arg_keys[6], 1), 0, BLOCK - 1).astype(jnp.int32)
    pair_count = with_ends(jax.random.randint(arg_keys[7], (TBLOCKS, FANOUT), 1, 9), jax.random.fold_in(arg_keys[7], 1), 1, 8).astype(jnp.int32)
    return dict(teacher_hidden=teacher_hidden, teacher_head=teacher_head, student_hidden=student_hidden, student_head=student_head, pair_owner=pair_owner, pair_block=pair_block, pair_shift=pair_shift, pair_count=pair_count)


kernel_decay = 0.8
loss_scale = 256.0


def kernel_table(offsets):
    offsets = jnp.asarray(offsets)[..., None, None]
    row_index = jnp.arange(BLOCK, dtype=jnp.int32)[:, None]
    col_index = jnp.arange(BLOCK, dtype=jnp.int32)[None, :]
    distance = (row_index - col_index + offsets) % BLOCK
    distance = jnp.minimum(distance, BLOCK - distance)
    return jnp.power(jnp.float32(kernel_decay), distance.astype(jnp.float32)).astype(jnp.bfloat16)


def reference(teacher_hidden, teacher_head, student_hidden, student_head, pair_owner, pair_block, pair_shift, pair_count):
    logits = jnp.dot(teacher_hidden, teacher_head, preferred_element_type=jnp.float32)
    row_peak = jnp.max(logits, axis=1, keepdims=True)
    teacher_probs = jnp.exp(logits - row_peak).astype(jnp.bfloat16)
    flat_probs = teacher_probs.reshape(TOKENS * TBLOCKS, BLOCK)
    base_table = kernel_table(jnp.zeros((), jnp.int32))
    smoothed = jnp.dot(flat_probs, base_table, preferred_element_type=jnp.float32)
    pair_tiles = smoothed.astype(jnp.bfloat16).reshape(TOKENS, TBLOCKS, BLOCK)
    teacher_ids = jnp.arange(TBLOCKS * FANOUT, dtype=jnp.int32) // FANOUT
    student_ids = (pair_owner * SB_DEV + pair_block).reshape(-1).astype(jnp.int32)
    shift_ids = pair_shift.reshape(-1).astype(jnp.int32)
    count_ids = pair_count.reshape(-1)

    def add_pair(running, pair_item):
        teacher_id, student_id, shift_id, count_id = pair_item
        tile_values = lax.dynamic_index_in_dim(pair_tiles, teacher_id, 1, keepdims=False)
        tile_values = jnp.roll(tile_values, shift_id, axis=1).astype(jnp.float32)
        current = lax.dynamic_index_in_dim(running, student_id, 1, keepdims=False)
        updated = current + count_id.astype(jnp.float32) * tile_values
        return lax.dynamic_update_index_in_dim(running, updated, student_id, 1), None

    zeros_init = jnp.zeros((TOKENS, SB_DEV * N_VOC, BLOCK), jnp.float32)
    aligned, _ = lax.scan(add_pair, zeros_init, (teacher_ids, student_ids, shift_ids, count_ids))
    aligned = aligned.reshape(TOKENS, SB_DEV * N_VOC * BLOCK)
    student_logits = jnp.dot(student_hidden, student_head, preferred_element_type=jnp.float32)
    student_top = jnp.max(student_logits, axis=1)
    student_total = jnp.sum(jnp.exp(student_logits - student_top[:, None]), axis=1)
    log_total = student_top + jnp.log(student_total)
    target_norm = jnp.sum(aligned, axis=1)
    target_cross = jnp.sum(aligned * student_logits, axis=1)
    token_loss = log_total - target_cross / target_norm
    logit_grad = (loss_scale * (jnp.exp(student_logits - log_total[:, None]) - aligned / target_norm[:, None])).astype(jnp.bfloat16)
    hidden_grad = jnp.dot(logit_grad, student_head.T, preferred_element_type=jnp.float32).astype(jnp.bfloat16)
    return (token_loss, hidden_grad)
```

```python
import jax
import jax.numpy as jnp
from jax import lax
from jax.experimental import pallas as pl
from jax.experimental.pallas import tpu as pltpu
from jax.sharding import Mesh
from jax.sharding import PartitionSpec as P

BLOCK = 128
TB_DEV = 8
SB_DEV = 10
FANOUT = 8
N_VOC = 64
NX, NC, NZ, NY = 4, 2, 16, 4
TBLOCKS = N_VOC * TB_DEV
SBLOCKS = N_VOC * SB_DEV
OWN = 2
TCOLS = TB_DEV * BLOCK
SCOLS = SB_DEV * BLOCK

kernel_decay = 0.8
loss_scale = 256.0
F32 = jnp.float32
BF16 = jnp.bfloat16


def base_kernel():
    row_index = lax.broadcasted_iota(jnp.int32, (BLOCK, BLOCK), 0)
    col_index = lax.broadcasted_iota(jnp.int32, (BLOCK, BLOCK), 1)
    distance = (row_index - col_index) % BLOCK
    distance = jnp.minimum(distance, BLOCK - distance)
    return jnp.power(F32(kernel_decay), distance.astype(F32)).astype(BF16)


def three_parts(value):
    first = lax.reduce_precision(value, 8, 7)
    rest = value - first
    second = lax.reduce_precision(rest, 8, 7)
    third = rest - second
    return [first, second, third]


def pack_columns(values):
    parts = []
    for value in values:
        parts.extend(three_parts(value))
    lanes = lax.broadcasted_iota(jnp.int32, (values[0].shape[0], BLOCK), 1)
    packed = jnp.zeros((values[0].shape[0], BLOCK), F32)
    for place, part in enumerate(parts):
        packed = jnp.where(lanes == place, part[:, None], packed)
    return packed.astype(BF16)


def unpack_column(packed, place):
    spot = 3 * place
    cols = packed[:, spot : spot + 3].astype(F32)
    return (cols[:, 0:1] + cols[:, 1:2]) + cols[:, 2:3]


def align_kernel(recv_ref, table_ref, weight_ref, shift_ref, out_ref, rolled_ref):
    lanes = lax.broadcasted_iota(jnp.int32, (TBLOCKS, BLOCK), 1)
    out_lanes = lax.broadcasted_iota(jnp.int32, (N_VOC, BLOCK), 1)
    for t in range(OWN):
        extra = recv_ref[t, :, TCOLS:]
        peak = unpack_column(extra, 0)
        scale = jnp.exp(peak - jnp.max(peak, axis=0, keepdims=True))
        smooth = []
        for j in range(TB_DEV):
            probs = recv_ref[t, :, j * BLOCK : (j + 1) * BLOCK]
            tile = jnp.dot(probs, table_ref[...], preferred_element_type=F32) * scale
            smooth.append(tile.astype(BF16).astype(F32))
        smooth = jnp.concatenate(smooth, axis=0)
        for k in range(FANOUT):
            index = (lanes - shift_ref[:, k : k + 1]) & (BLOCK - 1)
            rolled = jnp.take_along_axis(smooth, index, axis=1)
            rolled_ref[k * TBLOCKS : (k + 1) * TBLOCKS, t * BLOCK : (t + 1) * BLOCK] = rolled.astype(BF16)
    aligned = jnp.dot(weight_ref[...], rolled_ref[...], preferred_element_type=F32)
    for t in range(OWN):
        mine = aligned[:, t * BLOCK : (t + 1) * BLOCK]
        norm = jnp.sum(jnp.sum(mine, axis=0, keepdims=True), axis=1, keepdims=True)
        mine = mine / norm
        for b in range(SB_DEV):
            out_ref[t, :, b * BLOCK : (b + 1) * BLOCK] = mine[b * N_VOC : (b + 1) * N_VOC, :].astype(BF16)
        extra = recv_ref[t, :, TCOLS:]
        top = unpack_column(extra, 1)
        total = unpack_column(extra, 2)
        joint_top = jnp.max(top, axis=0, keepdims=True)
        joint_total = jnp.sum(total * jnp.exp(top - joint_top), axis=0, keepdims=True)
        log_total = joint_top + jnp.log(joint_total)
        first = log_total.astype(BF16).astype(F32)
        rest = log_total - first
        second = rest.astype(BF16).astype(F32)
        third = rest - second
        packed = jnp.where(out_lanes == 0, first, jnp.where(out_lanes == 1, second, jnp.where(out_lanes == 2, third, 0.0)))
        out_ref[t, :, SCOLS:] = packed.astype(BF16)


def align(recv, table, weight, shift):
    return pl.pallas_call(
        align_kernel,
        out_shape=jax.ShapeDtypeStruct((OWN, N_VOC, SCOLS + BLOCK), BF16),
        scratch_shapes=[pltpu.VMEM((FANOUT * TBLOCKS, OWN * BLOCK), BF16)],
        compiler_params=pltpu.CompilerParams(vmem_limit_bytes=40 * 1024 * 1024),
        name="align",
    )(recv, table, weight, shift)


def exchange(value, axis):
    return lax.all_to_all(value, axis, split_axis=0, concat_axis=0, tiled=True)


def spread(value, axis, size):
    return exchange(jnp.broadcast_to(value[None], (size,) + value.shape), axis)


def by_source(pairs):
    return pairs.reshape(N_VOC, TB_DEV, FANOUT).transpose(1, 0, 2).reshape(TBLOCKS, FANOUT)


def body(
    teacher_hidden,
    teacher_head,
    student_hidden,
    student_head,
    pair_owner,
    pair_block,
    pair_shift,
    pair_count,
):
    tok_rows = student_hidden.shape[0]
    head_full = lax.all_gather(student_head, ("x", "c"), axis=0, tiled=True)

    rows = spread(teacher_hidden, "z", NZ)
    rows = spread(rows, "y", NY)
    rows = rows.transpose(1, 0, 2, 3).reshape(-1, teacher_hidden.shape[1])

    table = base_kernel()
    shift = by_source(pair_shift)
    place = by_source(pair_block * N_VOC + pair_owner).T.reshape(1, -1)
    count = by_source(pair_count).T.reshape(1, -1)
    weight = jnp.where(
        place == lax.broadcasted_iota(jnp.int32, (SBLOCKS, TBLOCKS * FANOUT), 0), count, 0
    ).astype(BF16)

    partial_logits = jnp.dot(rows, teacher_head, preferred_element_type=F32)
    logits = lax.psum_scatter(partial_logits, ("x", "c"), scatter_dimension=0, tiled=True)
    peak = jnp.max(logits, axis=1)
    probs = jnp.exp(logits - peak[:, None]).astype(BF16)

    student_logits = jnp.dot(student_hidden, head_full, preferred_element_type=F32)
    local_top = jnp.max(student_logits, axis=1)
    local_total = jnp.sum(jnp.exp(student_logits - local_top[:, None]), axis=1)

    outgoing = jnp.concatenate([probs, pack_columns([peak, local_top, local_total])], axis=1)
    received = exchange(outgoing.reshape(N_VOC, OWN, TCOLS + BLOCK), ("z", "y"))
    target = align(received.transpose(1, 0, 2), table, weight, shift)
    target = exchange(target.transpose(1, 0, 2), ("z", "y")).reshape(tok_rows, SCOLS + BLOCK)

    log_total = unpack_column(target[:, SCOLS:], 0)
    target = target[:, :SCOLS].astype(F32)
    local_cross = jnp.sum(target * student_logits, axis=1)
    logit_grad = (loss_scale * (jnp.exp(student_logits - log_total) - target)).astype(BF16)
    grad_terms = lax.dot_general(
        logit_grad, head_full, (((1,), (1,)), ((), ())), preferred_element_type=F32
    )
    width = grad_terms.shape[1]
    terms = jnp.concatenate(
        [grad_terms, jnp.broadcast_to(local_cross[:, None], (tok_rows, BLOCK))], axis=1
    )
    terms = exchange(terms.reshape(NY, tok_rows // NY, width + BLOCK), "y").sum(axis=0)
    terms = exchange(terms.reshape(NZ, OWN, width + BLOCK), "z").sum(axis=0)
    result = jnp.concatenate([terms[:, :width].astype(BF16), pack_columns([terms[:, width]])], axis=1)
    result = spread(result, "z", NZ).reshape(NZ * OWN, width + BLOCK)
    result = spread(result, "y", NY).reshape(tok_rows, width + BLOCK)
    token_loss = log_total - unpack_column(result[:, width:], 0)
    return (token_loss[:, 0], result[:, :width])


def solution(mesh):
    grid = Mesh(mesh.devices.reshape(NX, NC, NZ, NY), ("x", "c", "z", "y"))
    tok = ("x", "c")
    voc = ("z", "y")
    in_specs = (
        P(voc, tok),
        P(tok, voc),
        P(tok, None),
        P(tok, voc),
        P(),
        P(),
        P(),
        P(),
    )
    out_specs = (P(tok), P(tok, None))
    return jax.shard_map(body, mesh=grid, in_specs=in_specs, out_specs=out_specs, check_vma=False)
```

```python
import jax
import jax.numpy as jnp
from jax import lax
from jax.experimental import pallas as pl
from jax.experimental.pallas import tpu as pltpu
from jax.sharding import Mesh
from jax.sharding import PartitionSpec as P

BLOCK = 128
TB_DEV = 8
SB_DEV = 10
FANOUT = 8
N_VOC = 64
NX, NC, NZ, NY = 4, 2, 16, 4
TBLOCKS = N_VOC * TB_DEV
SBLOCKS = N_VOC * SB_DEV
OWN = 2
DS = 1536
PIECE = DS // (NX * NC)
ROWS = PIECE // N_VOC
TCOLS = TB_DEV * BLOCK
SCOLS = SB_DEV * BLOCK
WIDE = DS + BLOCK

kernel_decay = 0.8
loss_scale = 256.0
F32 = jnp.float32
BF16 = jnp.bfloat16
VMEM_BYTES = 24 * 1024 * 1024


def kernel_call(kernel, out_shape, scratch=(), name=None, spots=False, arrays=0):
    specs = {}
    if spots:
        whole = pl.BlockSpec(memory_space=pltpu.VMEM)
        specs = dict(in_specs=[pl.BlockSpec(memory_space=pltpu.SMEM)] + [whole] * arrays)
    return pl.pallas_call(
        kernel,
        out_shape=out_shape,
        scratch_shapes=list(scratch),
        compiler_params=pltpu.CompilerParams(vmem_limit_bytes=VMEM_BYTES),
        name=name,
        **specs,
    )


def base_kernel():
    row_index = lax.broadcasted_iota(jnp.int32, (BLOCK, BLOCK), 0)
    col_index = lax.broadcasted_iota(jnp.int32, (BLOCK, BLOCK), 1)
    distance = (row_index - col_index) % BLOCK
    distance = jnp.minimum(distance, BLOCK - distance)
    return jnp.power(F32(kernel_decay), distance.astype(F32)).astype(BF16)


def pull_kernel(head_ref, select_ref, shift_ref, count_ref, out_ref, stacked_ref):
    for r in range(ROWS):
        for b in range(SB_DEV):
            stacked_ref[b * N_VOC : (b + 1) * N_VOC, r * BLOCK : (r + 1) * BLOCK] = head_ref[
                r, :, b * BLOCK : (b + 1) * BLOCK
            ]
    lanes = lax.broadcasted_iota(jnp.int32, (TBLOCKS, BLOCK), 1)
    sums = [jnp.zeros((TBLOCKS, BLOCK), F32) for _ in range(ROWS)]
    for k in range(FANOUT):
        picked = jnp.dot(
            select_ref[k * TBLOCKS : (k + 1) * TBLOCKS, :], stacked_ref[...], preferred_element_type=F32
        )
        index = (lanes + shift_ref[:, k : k + 1]) & (BLOCK - 1)
        count = count_ref[:, k : k + 1].astype(F32)
        for r in range(ROWS):
            rolled = jnp.take_along_axis(picked[:, r * BLOCK : (r + 1) * BLOCK], index, axis=1)
            sums[r] = sums[r] + count * rolled
    for r in range(ROWS):
        for j in range(TB_DEV):
            out_ref[r, :, j * BLOCK : (j + 1) * BLOCK] = sums[r][j * N_VOC : (j + 1) * N_VOC, :].astype(BF16)


def with_stats(rows, peak, mass):
    lanes = lax.broadcasted_iota(jnp.int32, (rows, BLOCK), 1)
    return jnp.where(lanes == 0, peak, jnp.where(lanes == 1, mass, 0.0))


def put_rows(full_ref, spots_ref, step, core, value):
    x = (spots_ref[0] + step) % NX
    start = (x * NC + core) * PIECE
    full_ref[pl.ds(pl.multiple_of(start, 64), PIECE), :] = value


def student_kernel(spots_ref, hidden_ref, mine_ref, theirs_ref, out_ref, head_ref):
    c = spots_ref[1]
    for step in range(NX):
        rows = slice(step * PIECE, (step + 1) * PIECE)
        put_rows(head_ref, spots_ref, step, c, mine_ref[rows, :])
        put_rows(head_ref, spots_ref, step, 1 - c, theirs_ref[rows, :])
    head = head_ref[...]
    logits = jnp.dot(hidden_ref[...], head, preferred_element_type=F32)
    top = jnp.max(logits, axis=1, keepdims=True)
    probs = jnp.exp(logits - top)
    total = jnp.sum(probs, axis=1, keepdims=True)
    out_ref[:, :DS] = lax.dot_general(
        probs.astype(BF16), head, (((1,), (1,)), ((), ())), preferred_element_type=F32
    )
    out_ref[:, DS:] = with_stats(out_ref.shape[0], top, total)


def rows_kernel(spots_ref, own_ref, after_ref, before_ref, low_ref, high_ref, head_ref, far_ref, rest_ref, mine_ref, rows_ref, theirs_ref):
    x, c, y = spots_ref[0], spots_ref[1], spots_ref[2]
    part = own_ref.shape[0] // NZ
    half = NZ // 2
    for step, ref in ((0, own_ref), (1, after_ref), (3, before_ref), (2, None)):
        spot = (y + step) % NY
        for z in range(NZ):
            source, local = ref, z
            if ref is None:
                source, local = (low_ref, z) if z < half else (high_ref, z - half)
            start = pl.multiple_of((z * NY + spot) * part, 16)
            rows_ref[pl.ds(start, part), :] = source[local * part : (local + 1) * part, :]
    chunk = far_ref.shape[0]
    for place, step in enumerate((2, 1, 3, 0)):
        first = ((x + step) % NX) * NC
        spot = slice(place * chunk, (place + 1) * chunk)
        theirs_ref[spot, :] = rows_ref[pl.ds(pl.multiple_of((first + 1 - c) * chunk, chunk), chunk), :]
        mine_ref[spot, :] = rows_ref[pl.ds(pl.multiple_of((first + c) * chunk, chunk), chunk), :]
    product = jnp.dot(theirs_ref[...], head_ref[...], preferred_element_type=F32)
    far_ref[...] = product[:chunk, :]
    rest_ref[...] = product[chunk:, :]


def teacher_kernel(spots_ref, own_ref, prev_ref, next_ref, table_ref, weight_ref, near_ref, far_ref, their_near_ref, their_far_ref, out_ref, smooth_ref, pulled_ref):
    c = spots_ref[1]
    for place, step in enumerate((0, 1, 3)):
        rows = slice(place * PIECE, (place + 1) * PIECE)
        put_rows(pulled_ref, spots_ref, step, c, near_ref[rows, :])
        put_rows(pulled_ref, spots_ref, step, 1 - c, their_near_ref[rows, :])
    put_rows(pulled_ref, spots_ref, 2, c, far_ref[...])
    put_rows(pulled_ref, spots_ref, 2, 1 - c, their_far_ref[...])
    logits = own_ref[...] + prev_ref[...] + next_ref[...]
    peak = jnp.max(logits, axis=1, keepdims=True)
    probs = jnp.exp(logits - peak).astype(BF16)
    for j in range(TB_DEV):
        part = slice(j * BLOCK, (j + 1) * BLOCK)
        smooth_ref[:, part] = jnp.dot(probs[:, part], table_ref[...], preferred_element_type=F32).astype(BF16)
    smooth = smooth_ref[...]
    norm = jnp.sum(smooth.astype(F32) * weight_ref[...], axis=1, keepdims=True)
    out_ref[:, :DS] = lax.dot_general(
        smooth, pulled_ref[...], (((1,), (1,)), ((), ())), preferred_element_type=F32
    )
    out_ref[:, DS:] = with_stats(out_ref.shape[0], peak, norm)


def merged(parts_ref):
    number = parts_ref.shape[0]
    stats = [parts_ref[i, :, DS:] for i in range(number)]
    peak = stats[0][:, 0:1]
    for i in range(1, number):
        peak = jnp.maximum(peak, stats[i][:, 0:1])
    rows, mass = 0.0, 0.0
    for i in range(number):
        scale = jnp.exp(stats[i][:, 0:1] - peak)
        rows = rows + scale * parts_ref[i, :, :DS]
        mass = mass + scale * stats[i][:, 1:2]
    return rows, peak, mass


def merge_kernel(parts_ref, out_ref):
    rows, peak, mass = merged(parts_ref)
    out_ref[:, :DS] = rows
    out_ref[:, DS:] = with_stats(out_ref.shape[0], peak, mass)


def finish_kernel(student_ref, target_ref, hidden_ref, out_ref):
    student, top, total = merged(student_ref)
    target, _, norm = merged(target_ref)
    target = target / norm
    cross = jnp.sum(target * hidden_ref[...], axis=1, keepdims=True)
    loss = top + jnp.log(total) - cross
    out_ref[:, :DS] = (loss_scale * (student / total - target)).astype(BF16)
    first = loss.astype(BF16).astype(F32)
    second = (loss - first).astype(BF16).astype(F32)
    third = loss - first - second
    lanes = lax.broadcasted_iota(jnp.int32, (OWN, BLOCK), 1)
    packed = jnp.where(lanes == 0, first, jnp.where(lanes == 1, second, jnp.where(lanes == 2, third, 0.0)))
    out_ref[:, DS:] = packed.astype(BF16)


def exchange(value, axis):
    return lax.all_to_all(value, axis, split_axis=0, concat_axis=0, tiled=True)


def spread(value, axis, size):
    return exchange(jnp.broadcast_to(value[None], (size,) + value.shape), axis)


def send(value, axis, size, step):
    return lax.ppermute(value, axis, [(i, (i + step) % size) for i in range(size)])


def send_x(value, step):
    return send(value, "x", NX, step)


def send_c(value):
    return lax.ppermute(value, "c", [(0, 1), (1, 0)])


def around(piece, axis, size):
    half = piece.shape[0] // 2
    after = send(piece, axis, size, -1)
    before = send(piece, axis, size, 1)
    far_low = send(after[:half], axis, size, -1)
    far_high = send(before[half:], axis, size, 1)
    return after, before, far_low, far_high


def by_source(pairs):
    return pairs.reshape(N_VOC, TB_DEV, FANOUT).transpose(1, 0, 2).reshape(TBLOCKS, FANOUT)


def logit_parts(rows, head, spots):
    size, width = NZ * rows.shape[1], rows.shape[2]
    rows = rows.reshape(size, width)
    pieces = around(rows, "y", NY)
    chunk = size * NY // (NX * NC)
    far_theirs, theirs, mine = kernel_call(
        rows_kernel,
        (
            jax.ShapeDtypeStruct((chunk, TCOLS), F32),
            jax.ShapeDtypeStruct((3 * chunk, TCOLS), F32),
            jax.ShapeDtypeStruct((4 * chunk, width), BF16),
        ),
        [pltpu.VMEM((NY * size, width), BF16), pltpu.VMEM((4 * chunk, width), BF16)],
        "rows",
        True,
        6,
    )(spots, rows, *pieces, head)
    far_theirs = send_c(far_theirs)
    theirs = send_c(theirs)
    mine = jnp.dot(mine, head, preferred_element_type=F32)
    far = mine[:chunk] + far_theirs
    half = chunk // 2
    low = send_x(far[:half], 1)
    high = send_x(far[half:], -1)
    near = mine[chunk:] + theirs
    after = jnp.concatenate([near[:half] + low, near[half:chunk]], axis=0)
    before = jnp.concatenate([near[chunk : chunk + half], near[chunk + half : 2 * chunk] + high], axis=0)
    return near[2 * chunk :], send_x(after, 1), send_x(before, -1)


def body(
    teacher_hidden,
    teacher_head,
    student_hidden,
    student_head,
    pair_owner,
    pair_block,
    pair_shift,
    pair_count,
):
    tok_rows = student_hidden.shape[0]
    x = lax.axis_index("x")
    c = lax.axis_index("c")
    z = lax.axis_index("z")
    y = lax.axis_index("y")
    spots = jnp.stack([x, c, y]).astype(jnp.int32)

    shift = by_source(pair_shift)
    count = by_source(pair_count)
    place = by_source(pair_block * N_VOC + pair_owner).T.reshape(-1, 1)
    select = (
        place == lax.broadcasted_iota(jnp.int32, (TBLOCKS * FANOUT, SBLOCKS), 1)
    ).astype(BF16)
    split = exchange(student_head.reshape(N_VOC, ROWS, SCOLS), ("z", "y"))
    pulled = kernel_call(
        pull_kernel,
        jax.ShapeDtypeStruct((ROWS, N_VOC, TCOLS), BF16),
        [pltpu.VMEM((SBLOCKS, ROWS * BLOCK), BF16)],
        "pull",
    )(split.transpose(1, 0, 2), select, shift, count)
    rows = spread(teacher_hidden, "z", NZ)
    pulled, hidden = lax.optimization_barrier((pulled, student_hidden))
    pulled = exchange(pulled.transpose(1, 0, 2), ("z", "y")).reshape(PIECE, TCOLS)

    head_mine = jnp.concatenate(
        [student_head, send_x(student_head, -1), send_x(student_head, 2), send_x(student_head, 1)], axis=0
    )
    head_theirs = send_c(head_mine)
    wide = jax.ShapeDtypeStruct((tok_rows, WIDE), F32)
    short = jax.ShapeDtypeStruct((tok_rows // NY, WIDE), F32)
    student = kernel_call(
        student_kernel, wide, [pltpu.VMEM((DS, SCOLS), BF16)], "student", True, 3
    )(spots, hidden, head_mine, head_theirs)
    pulled, student = lax.optimization_barrier((pulled, student))
    student = exchange(student.reshape(NY, tok_rows // NY, WIDE), "y")
    student = kernel_call(merge_kernel, short, name="merge_student")(student)

    own, before, after = logit_parts(rows, teacher_head, spots)
    student, own = lax.optimization_barrier((student, own))
    student = exchange(student.reshape(NZ, OWN, WIDE), "z")

    near, prior, low, high = around(pulled, "x", NX)
    near = jnp.concatenate([pulled, near, prior], axis=0)
    far = jnp.concatenate([low, high], axis=0)
    table = base_kernel()
    weight = jnp.sum(pair_count, axis=1).reshape(N_VOC, TB_DEV)
    weight = lax.dynamic_index_in_dim(weight, z * NY + y, 0, keepdims=False).astype(F32)
    weight = jnp.broadcast_to(weight[:, None], (TB_DEV, BLOCK)).reshape(1, TCOLS)
    target = kernel_call(
        teacher_kernel,
        wide,
        [pltpu.VMEM((tok_rows, TCOLS), BF16), pltpu.VMEM((DS, TCOLS), BF16)],
        "teacher",
        True,
        9,
    )(spots, own, before, after, table, weight, near, far, send_c(near), send_c(far))
    student, target = lax.optimization_barrier((student, target))
    target = exchange(target.reshape(NY, tok_rows // NY, WIDE), "y")
    target = kernel_call(merge_kernel, short, name="merge_target")(target)
    target = exchange(target.reshape(NZ, OWN, WIDE), "z")

    mine = lax.dynamic_slice_in_dim(student_hidden, (y * NZ + z) * OWN, OWN, 0).astype(F32)
    result = kernel_call(
        finish_kernel, jax.ShapeDtypeStruct((OWN, WIDE), BF16), name="finish"
    )(student, target, mine)
    result = spread(result, "z", NZ).reshape(NZ * OWN, WIDE)
    result = spread(result, "y", NY).reshape(tok_rows, WIDE)
    loss = result[:, DS : DS + 3].astype(F32)
    token_loss = (loss[:, 0] + loss[:, 1]) + loss[:, 2]
    return (token_loss, result[:, :DS])


def solution(mesh):
    grid = Mesh(mesh.devices.reshape(NX, NC, NZ, NY), ("x", "c", "z", "y"))
    tok = ("x", "c")
    voc = ("z", "y")
    in_specs = (
        P(voc, tok),
        P(tok, voc),
        P(tok, None),
        P(tok, voc),
        P(),
        P(),
        P(),
        P(),
    )
    out_specs = (P(tok), P(tok, None))
    return jax.shard_map(body, mesh=grid, in_specs=in_specs, out_specs=out_specs, check_vma=False)
```

```python
import jax
import jax.numpy as jnp
from jax import lax
from jax.experimental import pallas as pl
from jax.experimental.pallas import tpu as pltpu
from jax.sharding import Mesh
from jax.sharding import PartitionSpec as P

BLOCK = 128
TB_DEV = 8
SB_DEV = 10
FANOUT = 8
N_VOC = 64
NX, NC, NZ, NY = 4, 2, 16, 4
TBLOCKS = N_VOC * TB_DEV
SBLOCKS = N_VOC * SB_DEV
OWN = 2
DS = 1536
PIECE = DS // (NX * NC)
TCOLS = TB_DEV * BLOCK
SCOLS = SB_DEV * BLOCK
WIDE = DS + BLOCK

kernel_decay = 0.8
loss_scale = 256.0
F32 = jnp.float32
BF16 = jnp.bfloat16
VMEM_BYTES = 24 * 1024 * 1024
WHOLE_VMEM = 60 * 1024 * 1024


def kernel_call(kernel, out_shape, scratch=(), name=None, inputs=""):
    spaces = {"s": pltpu.SMEM, "v": pltpu.VMEM, "h": pl.ANY}
    return pl.pallas_call(
        kernel,
        out_shape=out_shape,
        in_specs=[pl.BlockSpec(memory_space=spaces[kind]) for kind in inputs],
        scratch_shapes=list(scratch),
        compiler_params=pltpu.CompilerParams(vmem_limit_bytes=WHOLE_VMEM if "h" in inputs else VMEM_BYTES),
        name=name,
    )


def arriving(array, dtype=BF16):
    return [pltpu.VMEM(array, dtype), pltpu.SemaphoreType.DMA]


def base_kernel():
    row_index = lax.broadcasted_iota(jnp.int32, (BLOCK, BLOCK), 0)
    col_index = lax.broadcasted_iota(jnp.int32, (BLOCK, BLOCK), 1)
    distance = (row_index - col_index) % BLOCK
    distance = jnp.minimum(distance, BLOCK - distance)
    return jnp.power(F32(kernel_decay), distance.astype(F32)).astype(BF16)


def split_parts(value):
    first = value.astype(BF16).astype(F32)
    second = (value - first).astype(BF16).astype(F32)
    return first, second, value - first - second


def pack_lanes(rows, values):
    lanes = lax.broadcasted_iota(jnp.int32, (rows, BLOCK), 1)
    packed = jnp.zeros((rows, BLOCK), F32)
    for place, value in enumerate(values):
        for step, part in enumerate(split_parts(value)):
            packed = jnp.where(lanes == 3 * place + step, part, packed)
    return packed.astype(BF16)


def unpack_lane(packed, place):
    spot = 3 * place
    cols = packed[:, spot : spot + 3].astype(F32)
    return (cols[:, 0:1] + cols[:, 1:2]) + cols[:, 2:3]


def put_rows(full_ref, spots_ref, step, core, value):
    x = (spots_ref[0] + step) % NX
    start = (x * NC + core) * PIECE
    full_ref[pl.ds(pl.multiple_of(start, 64), PIECE), :] = value


def student_kernel(spots_ref, hidden_ref, mine_ref, theirs_ref, head_ref, logits_ref, stats_ref):
    c = spots_ref[1]
    for step in range(NX):
        rows = slice(step * PIECE, (step + 1) * PIECE)
        put_rows(head_ref, spots_ref, step, c, mine_ref[rows, :])
        put_rows(head_ref, spots_ref, step, 1 - c, theirs_ref[rows, :])
    logits = jnp.dot(hidden_ref[...], head_ref[...], preferred_element_type=F32)
    top = jnp.max(logits, axis=1, keepdims=True)
    total = jnp.sum(jnp.exp(logits - top), axis=1, keepdims=True)
    logits_ref[...] = logits
    lanes = lax.broadcasted_iota(jnp.int32, stats_ref.shape, 1)
    stats_ref[...] = jnp.where(lanes == 0, top, total)


def rows_kernel(spots_ref, gathered_ref, head_ref, far_ref, rest_ref, mine_ref, rows_ref, theirs_ref):
    x, c = spots_ref[0], spots_ref[1]
    part = gathered_ref.shape[0] // (NZ * NY)
    for spot in range(NY):
        for z in range(NZ):
            rows_ref[(z * NY + spot) * part : (z * NY + spot + 1) * part, :] = gathered_ref[
                (spot * NZ + z) * part : (spot * NZ + z + 1) * part, :
            ]
    chunk = far_ref.shape[0]
    for place, step in enumerate((2, 1, 3, 0)):
        first = ((x + step) % NX) * NC
        spot = slice(place * chunk, (place + 1) * chunk)
        theirs_ref[spot, :] = rows_ref[pl.ds(pl.multiple_of((first + 1 - c) * chunk, chunk), chunk), :]
        mine_ref[spot, :] = rows_ref[pl.ds(pl.multiple_of((first + c) * chunk, chunk), chunk), :]
    product = jnp.dot(theirs_ref[...], head_ref[...], preferred_element_type=F32)
    far_ref[...] = product[:chunk, :]
    rest_ref[...] = product[chunk:, :]


def softmax_kernel(own_ref, prev_ref, next_ref, stats_ref, out_ref):
    logits = own_ref[...] + prev_ref[...] + next_ref[...]
    peak = jnp.max(logits, axis=1, keepdims=True)
    out_ref[:, :TCOLS] = jnp.exp(logits - peak).astype(BF16)
    out_ref[:, TCOLS:] = pack_lanes(out_ref.shape[0], [peak, stats_ref[:, 0:1], stats_ref[:, 1:2]])


def align_kernel(recv_ref, table_ref, source_ref, shift_ref, out_ref, rolled_ref, weight_ref, sem):
    copy = pltpu.make_async_copy(source_ref, weight_ref, sem)
    copy.start()
    lanes = lax.broadcasted_iota(jnp.int32, (TBLOCKS, BLOCK), 1)
    for t in range(OWN):
        extra = recv_ref[t, :, TCOLS:]
        peak = unpack_lane(extra, 0)
        scale = jnp.exp(peak - jnp.max(peak, axis=0, keepdims=True))
        smooth = []
        for j in range(TB_DEV):
            probs = recv_ref[t, :, j * BLOCK : (j + 1) * BLOCK]
            tile = jnp.dot(probs, table_ref[...], preferred_element_type=F32) * scale
            smooth.append(tile.astype(BF16).astype(F32))
        smooth = jnp.concatenate(smooth, axis=0)
        for k in range(FANOUT):
            index = (lanes - shift_ref[:, k : k + 1]) & (BLOCK - 1)
            rolled = jnp.take_along_axis(smooth, index, axis=1)
            rolled_ref[k * TBLOCKS : (k + 1) * TBLOCKS, t * BLOCK : (t + 1) * BLOCK] = rolled.astype(BF16)
    copy.wait()
    aligned = jnp.dot(weight_ref[...], rolled_ref[...], preferred_element_type=F32)
    for t in range(OWN):
        mine = aligned[:, t * BLOCK : (t + 1) * BLOCK]
        norm = jnp.sum(jnp.sum(mine, axis=0, keepdims=True), axis=1, keepdims=True)
        mine = mine / norm
        for b in range(SB_DEV):
            out_ref[t, :, b * BLOCK : (b + 1) * BLOCK] = mine[b * N_VOC : (b + 1) * N_VOC, :].astype(BF16)
        extra = recv_ref[t, :, TCOLS:]
        top = unpack_lane(extra, 1)
        total = unpack_lane(extra, 2)
        joint_top = jnp.max(top, axis=0, keepdims=True)
        joint_total = jnp.sum(total * jnp.exp(top - joint_top), axis=0, keepdims=True)
        log_total = joint_top + jnp.log(joint_total)
        out_ref[t, :, SCOLS:] = pack_lanes(N_VOC, [log_total])


def grad_kernel(target_ref, logits_ref, source_ref, out_ref, log_ref, head_ref, sem):
    copy = pltpu.make_async_copy(source_ref, head_ref, sem)
    copy.start()
    log_total = unpack_lane(target_ref[:, SCOLS:], 0)
    target = target_ref[:, :SCOLS].astype(F32)
    logits = logits_ref[...]
    cross = jnp.sum(target * logits, axis=1, keepdims=True)
    grad = (loss_scale * (jnp.exp(logits - log_total) - target)).astype(BF16)
    copy.wait()
    out_ref[:, :DS] = lax.dot_general(
        grad, head_ref[...], (((1,), (1,)), ((), ())), preferred_element_type=F32
    )
    out_ref[:, DS:] = jnp.broadcast_to(cross, (out_ref.shape[0], BLOCK))
    log_ref[...] = jnp.broadcast_to(log_total, log_ref.shape)


def finish_kernel(parts_ref, out_ref):
    terms = parts_ref[0]
    for i in range(1, NZ):
        terms = terms + parts_ref[i]
    out_ref[:, :DS] = terms[:, :DS].astype(BF16)
    out_ref[:, DS:] = pack_lanes(OWN, [terms[:, DS : DS + 1]])


def exchange(value, axis):
    return lax.all_to_all(value, axis, split_axis=0, concat_axis=0, tiled=True)


def spread(value, axis, size):
    return exchange(jnp.broadcast_to(value[None], (size,) + value.shape), axis)


def send(value, axis, size, step):
    return lax.ppermute(value, axis, [(i, (i + step) % size) for i in range(size)])


def send_x(value, step):
    return send(value, "x", NX, step)


def send_c(value):
    return lax.ppermute(value, "c", [(0, 1), (1, 0)])


def by_source(pairs):
    return pairs.reshape(N_VOC, TB_DEV, FANOUT).transpose(1, 0, 2).reshape(TBLOCKS, FANOUT)


def logit_parts(rows, head, spots):
    width = rows.shape[-1]
    rows = rows.reshape(-1, width)
    chunk = rows.shape[0] // (NX * NC)
    far_theirs, theirs, mine = kernel_call(
        rows_kernel,
        (
            jax.ShapeDtypeStruct((chunk, TCOLS), F32),
            jax.ShapeDtypeStruct((3 * chunk, TCOLS), F32),
            jax.ShapeDtypeStruct((4 * chunk, width), BF16),
        ),
        [pltpu.VMEM(rows.shape, BF16), pltpu.VMEM((4 * chunk, width), BF16)] ,
        "rows",
        "svv",
    )(spots, rows, head)
    far_theirs = send_c(far_theirs)
    theirs = send_c(theirs)
    mine = jnp.dot(mine, head, preferred_element_type=F32)
    far = mine[:chunk] + far_theirs
    half = chunk // 2
    low = send_x(far[:half], 1)
    high = send_x(far[half:], -1)
    near = mine[chunk:] + theirs
    after = jnp.concatenate([near[:half] + low, near[half:chunk]], axis=0)
    before = jnp.concatenate([near[chunk : chunk + half], near[chunk + half : 2 * chunk] + high], axis=0)
    return near[2 * chunk :], send_x(after, 1), send_x(before, -1)


def body(
    teacher_hidden,
    teacher_head,
    student_hidden,
    student_head,
    pair_owner,
    pair_block,
    pair_shift,
    pair_count,
):
    tok_rows = student_hidden.shape[0]
    spots = jnp.stack([lax.axis_index("x"), lax.axis_index("c")]).astype(jnp.int32)

    rows = spread(teacher_hidden, "z", NZ)
    head_mine = jnp.concatenate(
        [student_head, send_x(student_head, -1), send_x(student_head, 2), send_x(student_head, 1)], axis=0
    )
    head_theirs = send_c(head_mine)
    rows = spread(rows, "y", NY)

    shift = by_source(pair_shift)
    place = by_source(pair_block * N_VOC + pair_owner).T.reshape(1, -1)
    count = by_source(pair_count).T.reshape(1, -1)
    weight = jnp.where(
        place == lax.broadcasted_iota(jnp.int32, (SBLOCKS, TBLOCKS * FANOUT), 0), count, 0
    ).astype(BF16)

    head_full, student_logits, stats = kernel_call(
        student_kernel,
        (
            jax.ShapeDtypeStruct((DS, SCOLS), BF16),
            jax.ShapeDtypeStruct((tok_rows, SCOLS), F32),
            jax.ShapeDtypeStruct((tok_rows, BLOCK), F32),
        ),
        (),
        "student",
        "svvv",
    )(spots, student_hidden, head_mine, head_theirs)
    rows, weight, shift, stats = lax.optimization_barrier((rows, weight, shift, stats))

    own, before, after = logit_parts(rows, teacher_head, spots)
    outgoing = kernel_call(
        softmax_kernel, jax.ShapeDtypeStruct((tok_rows, TCOLS + BLOCK), BF16), name="softmax", inputs="vvvv"
    )(own, before, after, stats)
    received = exchange(outgoing.reshape(N_VOC, OWN, TCOLS + BLOCK), ("z", "y"))
    target = kernel_call(
        align_kernel,
        jax.ShapeDtypeStruct((OWN, N_VOC, SCOLS + BLOCK), BF16),
        [pltpu.VMEM((FANOUT * TBLOCKS, OWN * BLOCK), BF16)] + arriving((SBLOCKS, FANOUT * TBLOCKS)),
        "align",
        "vvhv",
    )(received.transpose(1, 0, 2), base_kernel(), weight, shift)
    target = exchange(target.transpose(1, 0, 2), ("z", "y")).reshape(tok_rows, SCOLS + BLOCK)

    terms, log_total = kernel_call(
        grad_kernel,
        (jax.ShapeDtypeStruct((tok_rows, WIDE), F32), jax.ShapeDtypeStruct((tok_rows, BLOCK), F32)),
        arriving((DS, SCOLS)),
        "gradient",
        "vvh",
    )(target, student_logits, head_full)
    terms = exchange(terms.reshape(NY, tok_rows // NY, WIDE), "y").sum(axis=0)
    terms = exchange(terms.reshape(NZ, OWN, WIDE), "z")
    result = kernel_call(
        finish_kernel, jax.ShapeDtypeStruct((OWN, WIDE), BF16), name="finish", inputs="v"
    )(terms)
    result = spread(result, "z", NZ).reshape(NZ * OWN, WIDE)
    result = spread(result, "y", NY).reshape(tok_rows, WIDE)
    token_loss = log_total[:, 0] - unpack_lane(result[:, DS:], 0)[:, 0]
    return (token_loss, result[:, :DS])


def solution(mesh):
    grid = Mesh(mesh.devices.reshape(NX, NC, NZ, NY), ("x", "c", "z", "y"))
    tok = ("x", "c")
    voc = ("z", "y")
    in_specs = (
        P(voc, tok),
        P(tok, voc),
        P(tok, None),
        P(tok, voc),
        P(),
        P(),
        P(),
        P(),
    )
    out_specs = (P(tok), P(tok, None))
    return jax.shard_map(body, mesh=grid, in_specs=in_specs, out_specs=out_specs, check_vma=False)
```

```python
import jax
import jax.numpy as jnp
from jax import lax
from jax.experimental import pallas as pl
from jax.experimental.pallas import tpu as pltpu
from jax.sharding import Mesh
from jax.sharding import PartitionSpec as P

BLOCK = 128
TB_DEV = 8
SB_DEV = 10
FANOUT = 8
N_VOC = 64
NX, NC, NZ, NY = 4, 2, 16, 4
TBLOCKS = N_VOC * TB_DEV
SBLOCKS = N_VOC * SB_DEV
OWN = 2
GROUP = 8
DS = 1536
PIECE = DS // (NX * NC)
TCOLS = TB_DEV * BLOCK
SCOLS = SB_DEV * BLOCK
WIDE = DS + BLOCK

kernel_decay = 0.8
loss_scale = 256.0
F32 = jnp.float32
BF16 = jnp.bfloat16
VMEM_BYTES = 28 * 1024 * 1024
WHOLE_VMEM = 60 * 1024 * 1024


def kernel_call(kernel, out_shape, scratch=(), name=None, inputs=""):
    spaces = {"s": pltpu.SMEM, "v": pltpu.VMEM, "h": pl.ANY}
    return pl.pallas_call(
        kernel,
        out_shape=out_shape,
        in_specs=[pl.BlockSpec(memory_space=spaces[kind]) for kind in inputs],
        scratch_shapes=list(scratch),
        compiler_params=pltpu.CompilerParams(vmem_limit_bytes=WHOLE_VMEM if "h" in inputs else VMEM_BYTES),
        name=name,
    )


def arriving(array, dtype=BF16):
    return [pltpu.VMEM(array, dtype), pltpu.SemaphoreType.DMA]


def base_kernel():
    row_index = lax.broadcasted_iota(jnp.int32, (BLOCK, BLOCK), 0)
    col_index = lax.broadcasted_iota(jnp.int32, (BLOCK, BLOCK), 1)
    distance = (row_index - col_index) % BLOCK
    distance = jnp.minimum(distance, BLOCK - distance)
    return jnp.power(F32(kernel_decay), distance.astype(F32)).astype(BF16)


def split_parts(value):
    first = value.astype(BF16).astype(F32)
    second = (value - first).astype(BF16).astype(F32)
    return first, second, value - first - second


def pack_lanes(rows, values):
    lanes = lax.broadcasted_iota(jnp.int32, (rows, BLOCK), 1)
    packed = jnp.zeros((rows, BLOCK), F32)
    for place, value in enumerate(values):
        for step, part in enumerate(split_parts(value)):
            packed = jnp.where(lanes == 3 * place + step, part, packed)
    return packed.astype(BF16)


def unpack_lane(packed, place):
    spot = 3 * place
    cols = packed[:, spot : spot + 3].astype(F32)
    return (cols[:, 0:1] + cols[:, 1:2]) + cols[:, 2:3]


def put_rows(full_ref, spots_ref, step, core, value):
    x = (spots_ref[0] + step) % NX
    start = (x * NC + core) * PIECE
    full_ref[pl.ds(pl.multiple_of(start, 64), PIECE), :] = value


def student_kernel(spots_ref, hidden_ref, mine_ref, theirs_ref, head_ref, logits_ref, stats_ref):
    c = spots_ref[1]
    for step in range(NX):
        rows = slice(step * PIECE, (step + 1) * PIECE)
        put_rows(head_ref, spots_ref, step, c, mine_ref[rows, :])
        put_rows(head_ref, spots_ref, step, 1 - c, theirs_ref[rows, :])
    logits = jnp.dot(hidden_ref[...], head_ref[...], preferred_element_type=F32)
    top = jnp.max(logits, axis=1, keepdims=True)
    total = jnp.sum(jnp.exp(logits - top), axis=1, keepdims=True)
    logits_ref[...] = logits
    lanes = lax.broadcasted_iota(jnp.int32, stats_ref.shape, 1)
    stats_ref[...] = jnp.where(lanes == 0, top, total)


def rows_kernel(spots_ref, gathered_ref, head_ref, far_ref, rest_ref, mine_ref, rows_ref, theirs_ref):
    x, c = spots_ref[0], spots_ref[1]
    part = gathered_ref.shape[0] // (NZ * NY)
    for spot in range(NY):
        for z in range(NZ):
            rows_ref[(z * NY + spot) * part : (z * NY + spot + 1) * part, :] = gathered_ref[
                (spot * NZ + z) * part : (spot * NZ + z + 1) * part, :
            ]
    chunk = far_ref.shape[0]
    for place, step in enumerate((2, 1, 3, 0)):
        first = ((x + step) % NX) * NC
        spot = slice(place * chunk, (place + 1) * chunk)
        theirs_ref[spot, :] = rows_ref[pl.ds(pl.multiple_of((first + 1 - c) * chunk, chunk), chunk), :]
        mine_ref[spot, :] = rows_ref[pl.ds(pl.multiple_of((first + c) * chunk, chunk), chunk), :]
    product = jnp.dot(theirs_ref[...], head_ref[...], preferred_element_type=F32)
    far_ref[...] = product[:chunk, :]
    rest_ref[...] = product[chunk:, :]


def softmax_kernel(own_ref, prev_ref, next_ref, stats_ref, out_ref):
    logits = own_ref[...] + prev_ref[...] + next_ref[...]
    peak = jnp.max(logits, axis=1, keepdims=True)
    out_ref[:, :TCOLS] = jnp.exp(logits - peak).astype(BF16)
    out_ref[:, TCOLS:] = pack_lanes(out_ref.shape[0], [peak, stats_ref[:, 0:1], stats_ref[:, 1:2]])


def align_kernel(recv_ref, table_ref, weight_ref, index_ref, count_ref, out_ref, wide_ref, smooth_ref, rolled_ref):
    for y in range(NY):
        size = recv_ref.shape[1]
        for j in range(TB_DEV + 1):
            part = recv_ref[y, :, j * BLOCK : (j + 1) * BLOCK]
            wide_ref[j, y * size : (y + 1) * size, :] = part.astype(F32)
    norms, logs = [], []
    for t in range(GROUP):
        rows = [wide_ref[j, pl.ds(t, N_VOC, stride=GROUP), :] for j in range(TB_DEV + 1)]
        extra = rows[TB_DEV]
        peak = unpack_lane(extra, 0)
        scale = jnp.exp(peak - jnp.max(peak, axis=0, keepdims=True))
        blocks = jnp.concatenate(rows[:TB_DEV], axis=0)
        smooth = jnp.dot(blocks.astype(BF16), table_ref[...], preferred_element_type=F32)
        smooth = (smooth * jnp.concatenate([scale] * TB_DEV, axis=0)).astype(BF16).astype(F32)
        smooth_ref[t] = smooth
        mass = jnp.sum(smooth * count_ref[...], axis=0, keepdims=True)
        norms.append(jnp.sum(mass, axis=1, keepdims=True))
        top = unpack_lane(extra, 1)
        total = unpack_lane(extra, 2)
        joint_top = jnp.max(top, axis=0, keepdims=True)
        joint_total = jnp.sum(total * jnp.exp(top - joint_top), axis=0, keepdims=True)
        logs.append(joint_top + jnp.log(joint_total))

    def roll(k, carry):
        index = index_ref[k]
        for t in range(GROUP):
            rolled = jnp.take_along_axis(smooth_ref[t], index, axis=1)
            start = pl.multiple_of(k * TBLOCKS, TBLOCKS)
            rolled_ref[pl.ds(start, TBLOCKS), t * BLOCK : (t + 1) * BLOCK] = rolled.astype(BF16)
        return carry

    lax.fori_loop(0, FANOUT, roll, 0)
    aligned = jnp.dot(weight_ref[...], rolled_ref[...], preferred_element_type=F32)
    for t in range(GROUP):
        mine = aligned[:, t * BLOCK : (t + 1) * BLOCK] / norms[t]
        for b in range(SB_DEV):
            out_ref[t, :, b * BLOCK : (b + 1) * BLOCK] = mine[b * NZ : (b + 1) * NZ, :].astype(BF16)
        out_ref[t, :, SCOLS:] = pack_lanes(NZ, [logs[t]])


def grad_kernel(target_ref, logits_ref, source_ref, out_ref, log_ref, head_ref, sem):
    copy = pltpu.make_async_copy(source_ref, head_ref, sem)
    copy.start()
    log_total = unpack_lane(target_ref[:, SCOLS:], 0)
    target = target_ref[:, :SCOLS].astype(F32)
    logits = logits_ref[...]
    cross = jnp.sum(target * logits, axis=1, keepdims=True)
    grad = (loss_scale * (jnp.exp(logits - log_total) - target)).astype(BF16)
    copy.wait()
    out_ref[:, :DS] = lax.dot_general(
        grad, head_ref[...], (((1,), (1,)), ((), ())), preferred_element_type=F32
    ).astype(BF16)
    out_ref[:, DS:] = pack_lanes(out_ref.shape[0], [cross])
    log_ref[...] = jnp.broadcast_to(log_total, log_ref.shape)


def finish_kernel(parts_ref, out_ref):
    terms = parts_ref[0]
    for i in range(1, NZ):
        terms = terms + parts_ref[i]
    out_ref[:, :DS] = terms[:, :DS].astype(BF16)
    cross = (terms[:, DS : DS + 1] + terms[:, DS + 1 : DS + 2]) + terms[:, DS + 2 : DS + 3]
    out_ref[:, DS:] = pack_lanes(OWN, [cross])


def exchange(value, axis):
    return lax.all_to_all(value, axis, split_axis=0, concat_axis=0, tiled=True)


def spread(value, axis, size):
    return exchange(jnp.broadcast_to(value[None], (size,) + value.shape), axis)


def send(value, axis, size, step):
    return lax.ppermute(value, axis, [(i, (i + step) % size) for i in range(size)])


def send_x(value, step):
    return send(value, "x", NX, step)


def send_c(value):
    return lax.ppermute(value, "c", [(0, 1), (1, 0)])


def by_source(pairs):
    pairs = pairs.reshape(NZ, NY, TB_DEV, FANOUT).transpose(2, 1, 0, 3)
    return pairs.reshape(TBLOCKS, FANOUT)


def logit_parts(rows, head, spots):
    width = rows.shape[-1]
    rows = rows.reshape(-1, width)
    chunk = rows.shape[0] // (NX * NC)
    far_theirs, theirs, mine = kernel_call(
        rows_kernel,
        (
            jax.ShapeDtypeStruct((chunk, TCOLS), F32),
            jax.ShapeDtypeStruct((3 * chunk, TCOLS), F32),
            jax.ShapeDtypeStruct((4 * chunk, width), BF16),
        ),
        [pltpu.VMEM(rows.shape, BF16), pltpu.VMEM((4 * chunk, width), BF16)] ,
        "rows",
        "svv",
    )(spots, rows, head)
    far_theirs = send_c(far_theirs)
    theirs = send_c(theirs)
    mine = jnp.dot(mine, head, preferred_element_type=F32)
    far = mine[:chunk] + far_theirs
    half = chunk // 2
    low = send_x(far[:half], 1)
    high = send_x(far[half:], -1)
    near = mine[chunk:] + theirs
    after = jnp.concatenate([near[:half] + low, near[half:chunk]], axis=0)
    before = jnp.concatenate([near[chunk : chunk + half], near[chunk + half : 2 * chunk] + high], axis=0)
    return near[2 * chunk :], send_x(after, 1), send_x(before, -1)


def body(
    teacher_hidden,
    teacher_head,
    student_hidden,
    student_head,
    pair_owner,
    pair_block,
    pair_shift,
    pair_count,
):
    tok_rows = student_hidden.shape[0]
    spots = jnp.stack([lax.axis_index("x"), lax.axis_index("c")]).astype(jnp.int32)

    rows = spread(teacher_hidden, "z", NZ)
    pieces = [student_head, send_x(student_head, -1), send_x(student_head, 2), send_x(student_head, 1)]
    pieces = lax.optimization_barrier((rows, *pieces))[1:]
    head_mine = jnp.concatenate(pieces, axis=0)
    head_theirs = send_c(head_mine)
    rows = spread(rows, "y", NY)

    shift = by_source(pair_shift)
    count = by_source(pair_count)
    owner = by_source(pair_owner)
    place = by_source(pair_block) * NZ + owner // NY
    place = jnp.where(owner % NY == lax.axis_index("y"), place, -1)
    weight = jnp.where(
        place.T.reshape(1, -1) == lax.broadcasted_iota(jnp.int32, (NZ * SB_DEV, TBLOCKS * FANOUT), 0),
        count.T.reshape(1, -1),
        0,
    ).astype(BF16)
    lanes = lax.broadcasted_iota(jnp.int32, (FANOUT, TBLOCKS, BLOCK), 2)
    index = (lanes - shift.T[:, :, None]) & (BLOCK - 1)
    mass = jnp.broadcast_to(jnp.sum(count, axis=1, keepdims=True).astype(F32), (TBLOCKS, BLOCK))

    head_full, student_logits, stats = kernel_call(
        student_kernel,
        (
            jax.ShapeDtypeStruct((DS, SCOLS), BF16),
            jax.ShapeDtypeStruct((tok_rows, SCOLS), F32),
            jax.ShapeDtypeStruct((tok_rows, BLOCK), F32),
        ),
        (),
        "student",
        "svvv",
    )(spots, student_hidden, head_mine, head_theirs)
    rows, weight, index, mass = lax.optimization_barrier((rows, weight, index, mass))

    own, before, after = logit_parts(rows, teacher_head, spots)
    outgoing = kernel_call(
        softmax_kernel, jax.ShapeDtypeStruct((tok_rows, TCOLS + BLOCK), BF16), name="softmax", inputs="vvvv"
    )(own, before, after, stats)
    received = exchange(outgoing.reshape(NZ, GROUP, TCOLS + BLOCK), "z")
    received = spread(received.reshape(tok_rows, TCOLS + BLOCK), "y", NY)
    target = kernel_call(
        align_kernel,
        jax.ShapeDtypeStruct((GROUP, NZ, SCOLS + BLOCK), BF16),
        [
            pltpu.VMEM((TB_DEV + 1, N_VOC * GROUP, BLOCK), F32),
            pltpu.VMEM((GROUP, TBLOCKS, BLOCK), F32),
            pltpu.VMEM((FANOUT * TBLOCKS, GROUP * BLOCK), BF16),
        ],
        "align",
        "vvvvv",
    )(received, base_kernel(), weight, index, mass)
    target = exchange(target.transpose(1, 0, 2), "z").reshape(tok_rows, SCOLS + BLOCK)

    terms, log_total = kernel_call(
        grad_kernel,
        (jax.ShapeDtypeStruct((tok_rows, WIDE), BF16), jax.ShapeDtypeStruct((tok_rows, BLOCK), F32)),
        arriving((DS, SCOLS)),
        "gradient",
        "vvh",
    )(target, student_logits, head_full)
    terms = exchange(terms.reshape(NY, tok_rows // NY, WIDE), "y").astype(F32).sum(axis=0)
    terms = exchange(terms.reshape(NZ, OWN, WIDE), "z")
    result = kernel_call(
        finish_kernel, jax.ShapeDtypeStruct((OWN, WIDE), BF16), name="finish", inputs="v"
    )(terms)
    result = spread(result, "z", NZ).reshape(NZ * OWN, WIDE)
    result = spread(result, "y", NY).reshape(tok_rows, WIDE)
    token_loss = log_total[:, 0] - unpack_lane(result[:, DS:], 0)[:, 0]
    return (token_loss, result[:, :DS])


def solution(mesh):
    grid = Mesh(mesh.devices.reshape(NX, NC, NZ, NY), ("x", "c", "z", "y"))
    tok = ("x", "c")
    voc = ("z", "y")
    in_specs = (
        P(voc, tok),
        P(tok, voc),
        P(tok, None),
        P(tok, voc),
        P(),
        P(),
        P(),
        P(),
    )
    out_specs = (P(tok), P(tok, None))
    return jax.shard_map(body, mesh=grid, in_specs=in_specs, out_specs=out_specs, check_vma=False)
```

```python
import jax
import jax.numpy as jnp
from jax import lax
from jax.experimental import pallas as pl
from jax.experimental.pallas import tpu as pltpu
from jax.sharding import Mesh
from jax.sharding import PartitionSpec as P

BLOCK = 128
TB_DEV = 8
SB_DEV = 10
FANOUT = 8
N_VOC = 64
NX, NC, NZ, NY = 4, 2, 16, 4
TBLOCKS = N_VOC * TB_DEV
SBLOCKS = N_VOC * SB_DEV
OWN = 2
DS = 1536
PIECE = DS // (NX * NC)
TCOLS = TB_DEV * BLOCK
SCOLS = SB_DEV * BLOCK
WIDE = DS + BLOCK

kernel_decay = 0.8
loss_scale = 256.0
F32 = jnp.float32
BF16 = jnp.bfloat16
VMEM_BYTES = 24 * 1024 * 1024
WHOLE_VMEM = 117 * 512 * 1024


def kernel_call(kernel, out_shape, scratch=(), name=None, inputs=""):
    spaces = {"s": pltpu.SMEM, "v": pltpu.VMEM, "h": pl.ANY}
    return pl.pallas_call(
        kernel,
        out_shape=out_shape,
        in_specs=[pl.BlockSpec(memory_space=spaces[kind]) for kind in inputs],
        scratch_shapes=list(scratch),
        compiler_params=pltpu.CompilerParams(vmem_limit_bytes=WHOLE_VMEM if "h" in inputs else VMEM_BYTES),
        name=name,
    )


def arriving(shape):
    return [pltpu.VMEM(shape, BF16), pltpu.SemaphoreType.DMA]


def base_kernel():
    row_index = lax.broadcasted_iota(jnp.int32, (BLOCK, BLOCK), 0)
    col_index = lax.broadcasted_iota(jnp.int32, (BLOCK, BLOCK), 1)
    distance = (row_index - col_index) % BLOCK
    distance = jnp.minimum(distance, BLOCK - distance)
    return jnp.power(F32(kernel_decay), distance.astype(F32)).astype(BF16)


def split_parts(value):
    first = value.astype(BF16).astype(F32)
    second = (value - first).astype(BF16).astype(F32)
    return first, second, value - first - second


def pack_lanes(rows, values):
    lanes = lax.broadcasted_iota(jnp.int32, (rows, BLOCK), 1)
    packed = jnp.zeros((rows, BLOCK), F32)
    for place, value in enumerate(values):
        for step, part in enumerate(split_parts(value)):
            packed = jnp.where(lanes == 3 * place + step, part, packed)
    return packed.astype(BF16)


def unpack_lane(packed, place):
    spot = 3 * place
    cols = packed[:, spot : spot + 3].astype(F32)
    return (cols[:, 0:1] + cols[:, 1:2]) + cols[:, 2:3]


def put_rows(full_ref, spots_ref, step, core, value):
    x = (spots_ref[0] + step) % NX
    start = (x * NC + core) * PIECE
    full_ref[pl.ds(pl.multiple_of(start, 64), PIECE), :] = value


def student_kernel(spots_ref, hidden_ref, mine_ref, theirs_ref, head_ref, logits_ref, stats_ref):
    c = spots_ref[1]
    for step in range(NX):
        rows = slice(step * PIECE, (step + 1) * PIECE)
        put_rows(head_ref, spots_ref, step, c, mine_ref[rows, :])
        put_rows(head_ref, spots_ref, step, 1 - c, theirs_ref[rows, :])
    logits = jnp.dot(hidden_ref[...], head_ref[...], preferred_element_type=F32)
    top = jnp.max(logits, axis=1, keepdims=True)
    total = jnp.sum(jnp.exp(logits - top), axis=1, keepdims=True)
    logits_ref[...] = logits
    lanes = lax.broadcasted_iota(jnp.int32, stats_ref.shape, 1)
    stats_ref[...] = jnp.where(lanes == 0, top, total)


def rows_kernel(spots_ref, gathered_ref, head_ref, far_ref, rest_ref, mine_ref, rows_ref, theirs_ref):
    x, c = spots_ref[0], spots_ref[1]
    part = gathered_ref.shape[0] // (NZ * NY)
    for spot in range(NY):
        for z in range(NZ):
            rows_ref[(z * NY + spot) * part : (z * NY + spot + 1) * part, :] = gathered_ref[
                (spot * NZ + z) * part : (spot * NZ + z + 1) * part, :
            ]
    chunk = far_ref.shape[0]
    for place, step in enumerate((2, 1, 3, 0)):
        first = ((x + step) % NX) * NC
        spot = slice(place * chunk, (place + 1) * chunk)
        theirs_ref[spot, :] = rows_ref[pl.ds(pl.multiple_of((first + 1 - c) * chunk, chunk), chunk), :]
        mine_ref[spot, :] = rows_ref[pl.ds(pl.multiple_of((first + c) * chunk, chunk), chunk), :]
    product = jnp.dot(theirs_ref[...], head_ref[...], preferred_element_type=F32)
    far_ref[...] = product[:chunk, :]
    rest_ref[...] = product[chunk:, :]


def softmax_kernel(own_ref, prev_ref, next_ref, stats_ref, out_ref):
    logits = own_ref[...] + prev_ref[...] + next_ref[...]
    peak = jnp.max(logits, axis=1, keepdims=True)
    out_ref[:, :TCOLS] = jnp.exp(logits - peak).astype(BF16)
    out_ref[:, TCOLS:] = pack_lanes(out_ref.shape[0], [peak, stats_ref[:, 0:1], stats_ref[:, 1:2]])


def weight_kernel(place_ref, count_ref, out_ref):
    place = place_ref[...]
    count = count_ref[...].astype(F32)
    for b in range(SB_DEV):
        rows = lax.broadcasted_iota(jnp.int32, (N_VOC, FANOUT * TBLOCKS), 0) + b * N_VOC
        out_ref[b * N_VOC : (b + 1) * N_VOC, :] = jnp.where(rows == place, count, 0.0).astype(BF16)


def align_kernel(recv_ref, table_ref, source_ref, shift_ref, out_ref, rolled_ref, weight_ref, sem):
    copy = pltpu.make_async_copy(source_ref, weight_ref, sem)
    copy.start()
    lanes = lax.broadcasted_iota(jnp.int32, (TBLOCKS, BLOCK), 1)
    for t in range(OWN):
        extra = recv_ref[t, :, TCOLS:]
        peak = unpack_lane(extra, 0)
        scale = jnp.exp(peak - jnp.max(peak, axis=0, keepdims=True))
        smooth = []
        for j in range(TB_DEV):
            probs = recv_ref[t, :, j * BLOCK : (j + 1) * BLOCK]
            tile = jnp.dot(probs, table_ref[...], preferred_element_type=F32) * scale
            smooth.append(tile.astype(BF16).astype(F32))
        smooth = jnp.concatenate(smooth, axis=0)
        for k in range(FANOUT):
            index = (lanes - shift_ref[:, k : k + 1]) & (BLOCK - 1)
            rolled = jnp.take_along_axis(smooth, index, axis=1)
            rolled_ref[k * TBLOCKS : (k + 1) * TBLOCKS, t * BLOCK : (t + 1) * BLOCK] = rolled.astype(BF16)
    copy.wait()
    aligned = jnp.dot(weight_ref[...], rolled_ref[...], preferred_element_type=F32)
    for t in range(OWN):
        mine = aligned[:, t * BLOCK : (t + 1) * BLOCK]
        norm = jnp.sum(jnp.sum(mine, axis=0, keepdims=True), axis=1, keepdims=True)
        mine = mine / norm
        for b in range(SB_DEV):
            out_ref[t, :, b * BLOCK : (b + 1) * BLOCK] = mine[b * N_VOC : (b + 1) * N_VOC, :].astype(BF16)
        extra = recv_ref[t, :, TCOLS:]
        top = unpack_lane(extra, 1)
        total = unpack_lane(extra, 2)
        joint_top = jnp.max(top, axis=0, keepdims=True)
        joint_total = jnp.sum(total * jnp.exp(top - joint_top), axis=0, keepdims=True)
        log_total = joint_top + jnp.log(joint_total)
        out_ref[t, :, SCOLS:] = pack_lanes(N_VOC, [log_total])


def grad_kernel(target_ref, logits_ref, source_ref, out_ref, log_ref, turned_ref, sem):
    copy = pltpu.make_async_copy(source_ref, turned_ref, sem)
    copy.start()
    log_total = unpack_lane(target_ref[:, SCOLS:], 0)
    target = target_ref[:, :SCOLS].astype(F32)
    logits = logits_ref[...]
    cross = jnp.sum(target * logits, axis=1, keepdims=True)
    grad = (loss_scale * (jnp.exp(logits - log_total) - target)).astype(BF16)
    copy.wait()
    out_ref[:, :DS] = jnp.dot(grad, turned_ref[...], preferred_element_type=F32)
    out_ref[:, DS:] = jnp.broadcast_to(cross, (out_ref.shape[0], BLOCK))
    log_ref[...] = jnp.broadcast_to(log_total, log_ref.shape)


def finish_kernel(parts_ref, out_ref):
    terms = parts_ref[0]
    for i in range(1, NZ):
        terms = terms + parts_ref[i]
    out_ref[:, :DS] = terms[:, :DS].astype(BF16)
    out_ref[:, DS:] = pack_lanes(OWN, [terms[:, DS : DS + 1]])


def exchange(value, axis):
    return lax.all_to_all(value, axis, split_axis=0, concat_axis=0, tiled=True)


def spread(value, axis, size):
    return exchange(jnp.broadcast_to(value[None], (size,) + value.shape), axis)


def send(value, axis, size, step):
    return lax.ppermute(value, axis, [(i, (i + step) % size) for i in range(size)])


def send_x(value, step):
    return send(value, "x", NX, step)


def send_c(value):
    return lax.ppermute(value, "c", [(0, 1), (1, 0)])


def by_source(pairs):
    return pairs.reshape(N_VOC, TB_DEV, FANOUT).transpose(1, 0, 2).reshape(TBLOCKS, FANOUT)


def logit_parts(rows, head, spots):
    width = rows.shape[-1]
    rows = rows.reshape(-1, width)
    chunk = rows.shape[0] // (NX * NC)
    far_theirs, theirs, mine = kernel_call(
        rows_kernel,
        (
            jax.ShapeDtypeStruct((chunk, TCOLS), F32),
            jax.ShapeDtypeStruct((3 * chunk, TCOLS), F32),
            jax.ShapeDtypeStruct((4 * chunk, width), BF16),
        ),
        [pltpu.VMEM(rows.shape, BF16), pltpu.VMEM((4 * chunk, width), BF16)] ,
        "rows",
        "svv",
    )(spots, rows, head)
    far_theirs = send_c(far_theirs)
    theirs = send_c(theirs)
    mine = jnp.dot(mine, head, preferred_element_type=F32)
    far = mine[:chunk] + far_theirs
    half = chunk // 2
    low = send_x(far[:half], 1)
    high = send_x(far[half:], -1)
    near = mine[chunk:] + theirs
    after = jnp.concatenate([near[:half] + low, near[half:chunk]], axis=0)
    before = jnp.concatenate([near[chunk : chunk + half], near[chunk + half : 2 * chunk] + high], axis=0)
    return near[2 * chunk :], send_x(after, 1), send_x(before, -1)


def body(
    teacher_hidden,
    teacher_head,
    student_hidden,
    student_head,
    pair_owner,
    pair_block,
    pair_shift,
    pair_count,
):
    tok_rows = student_hidden.shape[0]
    spots = jnp.stack([lax.axis_index("x"), lax.axis_index("c")]).astype(jnp.int32)

    rows = spread(teacher_hidden, "z", NZ)
    pieces = [student_head, send_x(student_head, -1), send_x(student_head, 2), send_x(student_head, 1)]
    pieces = lax.optimization_barrier((rows, *pieces))[1:]
    head_mine = jnp.concatenate(pieces, axis=0)
    head_theirs = send_c(head_mine)
    rows = spread(rows, "y", NY)

    shift = by_source(pair_shift)
    place = by_source(pair_block * N_VOC + pair_owner).T.reshape(1, -1)
    count = by_source(pair_count).T.reshape(1, -1)
    head_full, student_logits, stats = kernel_call(
        student_kernel,
        (
            jax.ShapeDtypeStruct((DS, SCOLS), BF16),
            jax.ShapeDtypeStruct((tok_rows, SCOLS), F32),
            jax.ShapeDtypeStruct((tok_rows, BLOCK), F32),
        ),
        (),
        "student",
        "svvv",
    )(spots, student_hidden, head_mine, head_theirs)
    rows, place, count, shift, stats = lax.optimization_barrier((rows, place, count, shift, stats))

    own, before, after = logit_parts(rows, teacher_head, spots)
    outgoing = kernel_call(
        softmax_kernel, jax.ShapeDtypeStruct((tok_rows, TCOLS + BLOCK), BF16), name="softmax", inputs="vvvv"
    )(own, before, after, stats)
    weight = kernel_call(
        weight_kernel,
        jax.ShapeDtypeStruct((SBLOCKS, FANOUT * TBLOCKS), BF16),
        name="weight",
        inputs="vv",
    )(place, count)
    received = exchange(outgoing.reshape(N_VOC, OWN, TCOLS + BLOCK), ("z", "y"))
    target = kernel_call(
        align_kernel,
        jax.ShapeDtypeStruct((OWN, N_VOC, SCOLS + BLOCK), BF16),
        [pltpu.VMEM((FANOUT * TBLOCKS, OWN * BLOCK), BF16)] + arriving(weight.shape),
        "align",
        "vvhv",
    )(received.transpose(1, 0, 2), base_kernel(), weight, shift)
    target = exchange(target.transpose(1, 0, 2), ("z", "y")).reshape(tok_rows, SCOLS + BLOCK)

    turned = head_full.T
    terms, log_total = kernel_call(
        grad_kernel,
        (jax.ShapeDtypeStruct((tok_rows, WIDE), F32), jax.ShapeDtypeStruct((tok_rows, BLOCK), F32)),
        arriving(turned.shape),
        "gradient",
        "vvh",
    )(target, student_logits, turned)
    terms = exchange(terms.reshape(NY, tok_rows // NY, WIDE), "y").sum(axis=0)
    terms = exchange(terms.reshape(NZ, OWN, WIDE), "z")
    result = kernel_call(
        finish_kernel, jax.ShapeDtypeStruct((OWN, WIDE), BF16), name="finish", inputs="v"
    )(terms)
    result = spread(result, "z", NZ).reshape(NZ * OWN, WIDE)
    result = spread(result, "y", NY).reshape(tok_rows, WIDE)
    token_loss = log_total[:, 0] - unpack_lane(result[:, DS:], 0)[:, 0]
    return (token_loss, result[:, :DS])


def solution(mesh):
    grid = Mesh(mesh.devices.reshape(NX, NC, NZ, NY), ("x", "c", "z", "y"))
    tok = ("x", "c")
    voc = ("z", "y")
    in_specs = (
        P(voc, tok),
        P(tok, voc),
        P(tok, None),
        P(tok, voc),
        P(),
        P(),
        P(),
        P(),
    )
    out_specs = (P(tok), P(tok, None))
    return jax.shard_map(body, mesh=grid, in_specs=in_specs, out_specs=out_specs, check_vma=False)
```

```python
import jax
import jax.numpy as jnp
from jax import lax
from jax.experimental import pallas as pl
from jax.experimental.pallas import tpu as pltpu
from jax.sharding import Mesh
from jax.sharding import PartitionSpec as P


BLOCK = 128
TB_DEV = 8
SB_DEV = 10
FANOUT = 8
N_VOC = 64
NX, NC, NZ, NY = 4, 2, 16, 4
TBLOCKS = N_VOC * TB_DEV
SBLOCKS = N_VOC * SB_DEV
OWN = 2
DS = 1536
PIECE = DS // (NX * NC)
TCOLS = TB_DEV * BLOCK
SCOLS = SB_DEV * BLOCK
WIDE = DS + BLOCK

kernel_decay = 0.8
loss_scale = 256.0
F32 = jnp.float32
BF16 = jnp.bfloat16
VMEM_BYTES = 24 * 1024 * 1024
WHOLE_VMEM = 117 * 512 * 1024


def kernel_call(kernel, out_shape, scratch=(), inputs=""):
    spaces = {"s": pltpu.SMEM, "v": pltpu.VMEM, "h": pl.ANY}
    return pl.pallas_call(
        kernel,
        out_shape=out_shape,
        in_specs=[pl.BlockSpec(memory_space=spaces[kind]) for kind in inputs],
        scratch_shapes=list(scratch),
        compiler_params=pltpu.CompilerParams(vmem_limit_bytes=WHOLE_VMEM if "h" in inputs else VMEM_BYTES),
    )


def arriving(shape):
    return [pltpu.VMEM(shape, BF16), pltpu.SemaphoreType.DMA]


def base_kernel():
    row_index = lax.broadcasted_iota(jnp.int32, (BLOCK, BLOCK), 0)
    col_index = lax.broadcasted_iota(jnp.int32, (BLOCK, BLOCK), 1)
    distance = (row_index - col_index) % BLOCK
    distance = jnp.minimum(distance, BLOCK - distance)
    return jnp.power(F32(kernel_decay), distance.astype(F32)).astype(BF16)


def split_parts(value):
    first = value.astype(BF16).astype(F32)
    second = (value - first).astype(BF16).astype(F32)
    return first, second, value - first - second


def pack_lanes(rows, values):
    lanes = lax.broadcasted_iota(jnp.int32, (rows, BLOCK), 1)
    packed = jnp.zeros((rows, BLOCK), F32)
    for place, value in enumerate(values):
        for step, part in enumerate(split_parts(value)):
            packed = jnp.where(lanes == 3 * place + step, part, packed)
    return packed.astype(BF16)


def unpack_lane(packed, place):
    spot = 3 * place
    cols = packed[:, spot : spot + 3].astype(F32)
    return (cols[:, 0:1] + cols[:, 1:2]) + cols[:, 2:3]


def put_rows(full_ref, spots_ref, step, core, value):
    x = (spots_ref[0] + step) % NX
    start = (x * NC + core) * PIECE
    full_ref[pl.ds(pl.multiple_of(start, 64), PIECE), :] = value


def student_kernel(spots_ref, hidden_ref, mine_ref, theirs_ref, head_ref, logits_ref, stats_ref):
    c = spots_ref[1]
    for place, step in enumerate((0, 1, 3, 2)):
        rows = slice(place * PIECE, (place + 1) * PIECE)
        put_rows(head_ref, spots_ref, step, c, mine_ref[rows, :])
        put_rows(head_ref, spots_ref, step, 1 - c, theirs_ref[rows, :])
    logits = jnp.dot(hidden_ref[...], head_ref[...], preferred_element_type=F32)
    top = jnp.max(logits, axis=1, keepdims=True)
    total = jnp.sum(jnp.exp(logits - top), axis=1, keepdims=True)
    logits_ref[...] = logits
    lanes = lax.broadcasted_iota(jnp.int32, stats_ref.shape, 1)
    stats_ref[...] = jnp.where(lanes == 0, top, total)


def rows_kernel(spots_ref, gathered_ref, head_ref, far_ref, rest_ref, mine_ref, rows_ref, theirs_ref):
    x, c = spots_ref[0], spots_ref[1]
    part = gathered_ref.shape[0] // (NZ * NY)
    for spot in range(NY):
        for z in range(NZ):
            rows_ref[(z * NY + spot) * part : (z * NY + spot + 1) * part, :] = gathered_ref[
                (spot * NZ + z) * part : (spot * NZ + z + 1) * part, :
            ]
    chunk = far_ref.shape[0]
    for place, step in enumerate((2, 1, 3, 0)):
        first = ((x + step) % NX) * NC
        spot = slice(place * chunk, (place + 1) * chunk)
        theirs_ref[spot, :] = rows_ref[pl.ds(pl.multiple_of((first + 1 - c) * chunk, chunk), chunk), :]
        mine_ref[spot, :] = rows_ref[pl.ds(pl.multiple_of((first + c) * chunk, chunk), chunk), :]
    product = jnp.dot(theirs_ref[...], head_ref[...], preferred_element_type=F32)
    far_ref[...] = product[:chunk, :]
    rest_ref[...] = product[chunk:, :]


def softmax_kernel(own_ref, prev_ref, next_ref, stats_ref, out_ref):
    logits = own_ref[...] + prev_ref[...] + next_ref[...]
    peak = jnp.max(logits, axis=1, keepdims=True)
    out_ref[:, :TCOLS] = jnp.exp(logits - peak).astype(BF16)
    out_ref[:, TCOLS:] = pack_lanes(out_ref.shape[0], [peak, stats_ref[:, 0:1], stats_ref[:, 1:2]])


def weight_kernel(place_ref, count_ref, out_ref):
    place = place_ref[...]
    count = count_ref[...].astype(F32)
    for b in range(SB_DEV):
        rows = lax.broadcasted_iota(jnp.int32, (N_VOC, FANOUT * TBLOCKS), 0) + b * N_VOC
        out_ref[b * N_VOC : (b + 1) * N_VOC, :] = jnp.where(rows == place, count, 0.0).astype(BF16)


def align_kernel(recv_ref, table_ref, source_ref, shift_ref, out_ref, rolled_ref, weight_ref, sem):
    copy = pltpu.make_async_copy(source_ref, weight_ref, sem)
    copy.start()
    lanes = lax.broadcasted_iota(jnp.int32, (TBLOCKS, BLOCK), 1)
    for t in range(OWN):
        extra = recv_ref[t, :, TCOLS:]
        peak = unpack_lane(extra, 0)
        scale = jnp.exp(peak - jnp.max(peak, axis=0, keepdims=True))
        smooth = []
        for j in range(TB_DEV):
            probs = recv_ref[t, :, j * BLOCK : (j + 1) * BLOCK]
            tile = jnp.dot(probs, table_ref[...], preferred_element_type=F32) * scale
            smooth.append(tile.astype(BF16).astype(F32))
        smooth = jnp.concatenate(smooth, axis=0)
        for k in range(FANOUT):
            index = (lanes - shift_ref[:, k : k + 1]) & (BLOCK - 1)
            rolled = jnp.take_along_axis(smooth, index, axis=1)
            rolled_ref[k * TBLOCKS : (k + 1) * TBLOCKS, t * BLOCK : (t + 1) * BLOCK] = rolled.astype(BF16)
    copy.wait()
    aligned = jnp.dot(weight_ref[...], rolled_ref[...], preferred_element_type=F32)
    for t in range(OWN):
        mine = aligned[:, t * BLOCK : (t + 1) * BLOCK]
        norm = jnp.sum(jnp.sum(mine, axis=0, keepdims=True), axis=1, keepdims=True)
        mine = mine / norm
        for b in range(SB_DEV):
            out_ref[t, :, b * BLOCK : (b + 1) * BLOCK] = mine[b * N_VOC : (b + 1) * N_VOC, :].astype(BF16)
        extra = recv_ref[t, :, TCOLS:]
        top = unpack_lane(extra, 1)
        total = unpack_lane(extra, 2)
        joint_top = jnp.max(top, axis=0, keepdims=True)
        joint_total = jnp.sum(total * jnp.exp(top - joint_top), axis=0, keepdims=True)
        log_total = joint_top + jnp.log(joint_total)
        out_ref[t, :, SCOLS:] = pack_lanes(N_VOC, [log_total])


def grad_kernel(target_ref, logits_ref, source_ref, out_ref, log_ref, turned_ref, sem):
    copy = pltpu.make_async_copy(source_ref, turned_ref, sem)
    copy.start()
    log_total = unpack_lane(target_ref[:, SCOLS:], 0)
    target = target_ref[:, :SCOLS].astype(F32)
    logits = logits_ref[...]
    cross = jnp.sum(target * logits, axis=1, keepdims=True)
    grad = (loss_scale * (jnp.exp(logits - log_total) - target)).astype(BF16)
    copy.wait()
    out_ref[:, :DS] = jnp.dot(grad, turned_ref[...], preferred_element_type=F32)
    out_ref[:, DS:] = jnp.broadcast_to(cross, (out_ref.shape[0], BLOCK))
    log_ref[...] = jnp.broadcast_to(log_total, log_ref.shape)


def finish_kernel(parts_ref, out_ref):
    terms = parts_ref[0]
    for i in range(1, NZ):
        terms = terms + parts_ref[i]
    out_ref[:, :DS] = terms[:, :DS].astype(BF16)
    out_ref[:, DS:] = pack_lanes(OWN, [terms[:, DS : DS + 1]])


def exchange(value, axis):
    return lax.all_to_all(value, axis, split_axis=0, concat_axis=0, tiled=True)


def spread(value, axis, size):
    return exchange(jnp.broadcast_to(value[None], (size,) + value.shape), axis)


def send(value, axis, size, step):
    return lax.ppermute(value, axis, [(i, (i + step) % size) for i in range(size)])


def send_x(value, step):
    return send(value, "x", NX, step)


def send_c(value):
    return lax.ppermute(value, "c", [(0, 1), (1, 0)])


def by_source(pairs):
    return pairs.reshape(N_VOC, TB_DEV, FANOUT).transpose(1, 0, 2).reshape(TBLOCKS, FANOUT)


def logit_parts(rows, head, spots):
    width = rows.shape[-1]
    rows = rows.reshape(-1, width)
    chunk = rows.shape[0] // (NX * NC)
    far_theirs, theirs, mine = kernel_call(
        rows_kernel,
        (
            jax.ShapeDtypeStruct((chunk, TCOLS), F32),
            jax.ShapeDtypeStruct((3 * chunk, TCOLS), F32),
            jax.ShapeDtypeStruct((4 * chunk, width), BF16),
        ),
        [pltpu.VMEM(rows.shape, BF16), pltpu.VMEM((4 * chunk, width), BF16)] ,
        "svv",
    )(spots, rows, head)
    far_theirs = send_c(far_theirs)
    theirs = send_c(theirs)
    mine = jnp.dot(mine, head, preferred_element_type=F32)
    far = mine[:chunk] + far_theirs
    half = chunk // 2
    low = send_x(far[:half], 1)
    high = send_x(far[half:], -1)
    near = mine[chunk:] + theirs
    after = jnp.concatenate([near[:half] + low, near[half:chunk]], axis=0)
    before = jnp.concatenate([near[chunk : chunk + half], near[chunk + half : 2 * chunk] + high], axis=0)
    return near[2 * chunk :], send_x(after, 1), send_x(before, -1)


def step(
    teacher_hidden,
    teacher_head,
    student_hidden,
    student_head,
    pair_owner,
    pair_block,
    pair_shift,
    pair_count,
):
    tok_rows = student_hidden.shape[0]
    spots = jnp.stack([lax.axis_index("x"), lax.axis_index("c")]).astype(jnp.int32)

    rows = spread(teacher_hidden, "z", NZ)
    pieces = [student_head, send_x(student_head, -1), send_x(student_head, 1), send_x(student_head, 2)]
    head_mine = jnp.concatenate(pieces, axis=0)
    head_theirs = send_c(head_mine)
    rows = spread(rows, "y", NY)

    shift = by_source(pair_shift)
    place = by_source(pair_block * N_VOC + pair_owner).T.reshape(1, -1)
    count = by_source(pair_count).T.reshape(1, -1)
    head_full, student_logits, stats = kernel_call(
        student_kernel,
        (
            jax.ShapeDtypeStruct((DS, SCOLS), BF16),
            jax.ShapeDtypeStruct((tok_rows, SCOLS), F32),
            jax.ShapeDtypeStruct((tok_rows, BLOCK), F32),
        ),
        (),
        "svvv",
    )(spots, student_hidden, head_mine, head_theirs)
    rows, place, count, shift, stats = lax.optimization_barrier((rows, place, count, shift, stats))

    own, before, after = logit_parts(rows, teacher_head, spots)
    outgoing = kernel_call(
        softmax_kernel, jax.ShapeDtypeStruct((tok_rows, TCOLS + BLOCK), BF16), inputs="vvvv"
    )(own, before, after, stats)
    weight = kernel_call(
        weight_kernel, jax.ShapeDtypeStruct((SBLOCKS, FANOUT * TBLOCKS), BF16), inputs="vv"
    )(place, count)
    received = exchange(outgoing.reshape(N_VOC, OWN, TCOLS + BLOCK), ("z", "y"))
    target = kernel_call(
        align_kernel,
        jax.ShapeDtypeStruct((OWN, N_VOC, SCOLS + BLOCK), BF16),
        [pltpu.VMEM((FANOUT * TBLOCKS, OWN * BLOCK), BF16)] + arriving(weight.shape),
        "vvhv",
    )(received.transpose(1, 0, 2), base_kernel(), weight, shift)
    target = exchange(target.transpose(1, 0, 2), ("z", "y")).reshape(tok_rows, SCOLS + BLOCK)

    turned = head_full.T
    terms, log_total = kernel_call(
        grad_kernel,
        (jax.ShapeDtypeStruct((tok_rows, WIDE), F32), jax.ShapeDtypeStruct((tok_rows, BLOCK), F32)),
        arriving(turned.shape),
        "vvh",
    )(target, student_logits, turned)
    terms = exchange(terms.reshape(NY, tok_rows // NY, WIDE), "y").sum(axis=0)
    terms = exchange(terms.reshape(NZ, OWN, WIDE), "z")
    result = kernel_call(finish_kernel, jax.ShapeDtypeStruct((OWN, WIDE), BF16), inputs="v")(terms)
    result = spread(result, "z", NZ).reshape(NZ * OWN, WIDE)
    result = spread(result, "y", NY).reshape(tok_rows, WIDE)
    token_loss = log_total[:, 0] - unpack_lane(result[:, DS:], 0)[:, 0]
    return (token_loss, result[:, :DS])


def solution(mesh):
    grid = Mesh(mesh.devices.reshape(NX, NC, NZ, NY), ("x", "c", "z", "y"))
    tok = ("x", "c")
    voc = ("z", "y")
    in_specs = (
        P(voc, tok),
        P(tok, voc),
        P(tok, None),
        P(tok, voc),
        P(),
        P(),
        P(),
        P(),
    )
    out_specs = (P(tok), P(tok, None))
    return jax.shard_map(step, mesh=grid, in_specs=in_specs, out_specs=out_specs, check_vma=False)
```

```python
import jax
import jax.numpy as jnp
from jax import lax
from jax.experimental import pallas as pl
from jax.experimental.pallas import tpu as pltpu
from jax.sharding import Mesh
from jax.sharding import PartitionSpec as P


BLOCK = 128
TB_DEV = 8
SB_DEV = 10
FANOUT = 8
N_VOC = 64
NX, NC, NZ, NY = 4, 2, 16, 4
TBLOCKS = N_VOC * TB_DEV
SBLOCKS = N_VOC * SB_DEV
OWN = 2
DS = 1536
PIECE = DS // (NX * NC)
TCOLS = TB_DEV * BLOCK
SCOLS = SB_DEV * BLOCK
WIDE = DS + BLOCK

kernel_decay = 0.8
loss_scale = 256.0
F32 = jnp.float32
BF16 = jnp.bfloat16
VMEM_BYTES = 24 * 1024 * 1024


def kernel_call(kernel, out_shape, scratch=(), inputs="", flops=0):
    spaces = {"s": pltpu.SMEM, "v": pltpu.VMEM}
    return pl.pallas_call(
        kernel,
        out_shape=out_shape,
        in_specs=[pl.BlockSpec(memory_space=spaces[kind]) for kind in inputs],
        scratch_shapes=list(scratch),
        compiler_params=pltpu.CompilerParams(vmem_limit_bytes=VMEM_BYTES),
        cost_estimate=pl.CostEstimate(flops=flops, bytes_accessed=1 << 20, transcendentals=0) if flops else None,
    )


def base_kernel():
    row_index = lax.broadcasted_iota(jnp.int32, (BLOCK, BLOCK), 0)
    col_index = lax.broadcasted_iota(jnp.int32, (BLOCK, BLOCK), 1)
    distance = (row_index - col_index) % BLOCK
    distance = jnp.minimum(distance, BLOCK - distance)
    return jnp.power(F32(kernel_decay), distance.astype(F32)).astype(BF16)


def split_parts(value):
    first = value.astype(BF16).astype(F32)
    second = (value - first).astype(BF16).astype(F32)
    return first, second, value - first - second


def pack_lanes(rows, values):
    lanes = lax.broadcasted_iota(jnp.int32, (rows, BLOCK), 1)
    packed = jnp.zeros((rows, BLOCK), F32)
    for place, value in enumerate(values):
        for step, part in enumerate(split_parts(value)):
            packed = jnp.where(lanes == 3 * place + step, part, packed)
    return packed.astype(BF16)


def unpack_lane(packed, place):
    spot = 3 * place
    cols = packed[:, spot : spot + 3].astype(F32)
    return (cols[:, 0:1] + cols[:, 1:2]) + cols[:, 2:3]


def put_rows(full_ref, spots_ref, step, core, value):
    x = (spots_ref[0] + step) % NX
    start = (x * NC + core) * PIECE
    full_ref[pl.ds(pl.multiple_of(start, 64), PIECE), :] = value


def student_kernel(spots_ref, hidden_ref, mine_ref, theirs_ref, head_ref, logits_ref, stats_ref):
    c = spots_ref[1]
    for place, step in enumerate((0, 1, 3, 2)):
        rows = slice(place * PIECE, (place + 1) * PIECE)
        put_rows(head_ref, spots_ref, step, c, mine_ref[rows, :])
        put_rows(head_ref, spots_ref, step, 1 - c, theirs_ref[rows, :])
    logits = jnp.dot(hidden_ref[...], head_ref[...], preferred_element_type=F32)
    top = jnp.max(logits, axis=1, keepdims=True)
    total = jnp.sum(jnp.exp(logits - top), axis=1, keepdims=True)
    logits_ref[...] = logits
    lanes = lax.broadcasted_iota(jnp.int32, stats_ref.shape, 1)
    stats_ref[...] = jnp.where(lanes == 0, top, total)


def rows_kernel(spots_ref, gathered_ref, head_ref, far_ref, rest_ref, mine_ref, rows_ref, theirs_ref):
    x, c = spots_ref[0], spots_ref[1]
    part = gathered_ref.shape[0] // (NZ * NY)
    for spot in range(NY):
        for z in range(NZ):
            rows_ref[(z * NY + spot) * part : (z * NY + spot + 1) * part, :] = gathered_ref[
                (spot * NZ + z) * part : (spot * NZ + z + 1) * part, :
            ]
    chunk = far_ref.shape[0]
    for place, step in enumerate((2, 1, 3, 0)):
        first = ((x + step) % NX) * NC
        spot = slice(place * chunk, (place + 1) * chunk)
        theirs_ref[spot, :] = rows_ref[pl.ds(pl.multiple_of((first + 1 - c) * chunk, chunk), chunk), :]
        mine_ref[spot, :] = rows_ref[pl.ds(pl.multiple_of((first + c) * chunk, chunk), chunk), :]
    product = jnp.dot(theirs_ref[...], head_ref[...], preferred_element_type=F32)
    far_ref[...] = product[:chunk, :]
    rest_ref[...] = product[chunk:, :]


def softmax_kernel(own_ref, prev_ref, next_ref, stats_ref, out_ref):
    logits = own_ref[...] + prev_ref[...] + next_ref[...]
    peak = jnp.max(logits, axis=1, keepdims=True)
    out_ref[:, :TCOLS] = jnp.exp(logits - peak).astype(BF16)
    out_ref[:, TCOLS:] = pack_lanes(out_ref.shape[0], [peak, stats_ref[:, 0:1], stats_ref[:, 1:2]])


def weight_kernel(place_ref, count_ref, out_ref):
    place = place_ref[...]
    count = count_ref[...].astype(F32)
    for b in range(SB_DEV):
        rows = lax.broadcasted_iota(jnp.int32, (N_VOC, FANOUT * TBLOCKS), 0) + b * N_VOC
        out_ref[b * N_VOC : (b + 1) * N_VOC, :] = jnp.where(rows == place, count, 0.0).astype(BF16)


def roll_kernel(recv_ref, table_ref, shift_ref, rolled_ref):
    lanes = lax.broadcasted_iota(jnp.int32, (TBLOCKS, BLOCK), 1)
    for t in range(OWN):
        extra = recv_ref[t, :, TCOLS:]
        peak = unpack_lane(extra, 0)
        scale = jnp.exp(peak - jnp.max(peak, axis=0, keepdims=True))
        smooth = []
        for j in range(TB_DEV):
            probs = recv_ref[t, :, j * BLOCK : (j + 1) * BLOCK]
            tile = jnp.dot(probs, table_ref[...], preferred_element_type=F32) * scale
            smooth.append(tile.astype(BF16).astype(F32))
        smooth = jnp.concatenate(smooth, axis=0)
        for k in range(FANOUT):
            index = (lanes - shift_ref[:, k : k + 1]) & (BLOCK - 1)
            rolled = jnp.take_along_axis(smooth, index, axis=1)
            rolled_ref[k * TBLOCKS : (k + 1) * TBLOCKS, t * BLOCK : (t + 1) * BLOCK] = rolled.astype(BF16)


def align_kernel(recv_ref, rolled_ref, weight_ref, out_ref):
    aligned = jnp.dot(weight_ref[...], rolled_ref[...], preferred_element_type=F32)
    for t in range(OWN):
        mine = aligned[:, t * BLOCK : (t + 1) * BLOCK]
        norm = jnp.sum(jnp.sum(mine, axis=0, keepdims=True), axis=1, keepdims=True)
        mine = mine / norm
        for b in range(SB_DEV):
            out_ref[t, :, b * BLOCK : (b + 1) * BLOCK] = mine[b * N_VOC : (b + 1) * N_VOC, :].astype(BF16)
        extra = recv_ref[t, :, TCOLS:]
        top = unpack_lane(extra, 1)
        total = unpack_lane(extra, 2)
        joint_top = jnp.max(top, axis=0, keepdims=True)
        joint_total = jnp.sum(total * jnp.exp(top - joint_top), axis=0, keepdims=True)
        log_total = joint_top + jnp.log(joint_total)
        out_ref[t, :, SCOLS:] = pack_lanes(N_VOC, [log_total])


def grad_kernel(target_ref, logits_ref, grad_ref, cross_ref, log_ref):
    log_total = unpack_lane(target_ref[:, SCOLS:], 0)
    target = target_ref[:, :SCOLS].astype(F32)
    logits = logits_ref[...]
    cross = jnp.sum(target * logits, axis=1, keepdims=True)
    grad_ref[...] = (loss_scale * (jnp.exp(logits - log_total) - target)).astype(BF16)
    cross_ref[...] = jnp.broadcast_to(cross, cross_ref.shape)
    log_ref[...] = jnp.broadcast_to(log_total, log_ref.shape)


def terms_kernel(grad_ref, turned_ref, cross_ref, out_ref):
    out_ref[:, :DS] = jnp.dot(grad_ref[...], turned_ref[...], preferred_element_type=F32)
    out_ref[:, DS:] = cross_ref[...]


def finish_kernel(parts_ref, out_ref):
    terms = parts_ref[0]
    for i in range(1, NZ):
        terms = terms + parts_ref[i]
    out_ref[:, :DS] = terms[:, :DS].astype(BF16)
    out_ref[:, DS:] = pack_lanes(OWN, [terms[:, DS : DS + 1]])


def exchange(value, axis):
    return lax.all_to_all(value, axis, split_axis=0, concat_axis=0, tiled=True)


def spread(value, axis, size):
    return exchange(jnp.broadcast_to(value[None], (size,) + value.shape), axis)


def send(value, axis, size, step):
    return lax.ppermute(value, axis, [(i, (i + step) % size) for i in range(size)])


def send_x(value, step):
    return send(value, "x", NX, step)


def send_c(value):
    return lax.ppermute(value, "c", [(0, 1), (1, 0)])


def by_source(pairs):
    return pairs.reshape(N_VOC, TB_DEV, FANOUT).transpose(1, 0, 2).reshape(TBLOCKS, FANOUT)


def logit_parts(rows, head, spots):
    width = rows.shape[-1]
    rows = rows.reshape(-1, width)
    chunk = rows.shape[0] // (NX * NC)
    far_theirs, theirs, mine = kernel_call(
        rows_kernel,
        (
            jax.ShapeDtypeStruct((chunk, TCOLS), F32),
            jax.ShapeDtypeStruct((3 * chunk, TCOLS), F32),
            jax.ShapeDtypeStruct((4 * chunk, width), BF16),
        ),
        [pltpu.VMEM(rows.shape, BF16), pltpu.VMEM((4 * chunk, width), BF16)] ,
        "svv",
    )(spots, rows, head)
    far_theirs = send_c(far_theirs)
    theirs = send_c(theirs)
    mine = jnp.dot(mine, head, preferred_element_type=F32)
    far = mine[:chunk] + far_theirs
    half = chunk // 2
    low = send_x(far[:half], 1)
    high = send_x(far[half:], -1)
    near = mine[chunk:] + theirs
    after = jnp.concatenate([near[:half] + low, near[half:chunk]], axis=0)
    before = jnp.concatenate([near[chunk : chunk + half], near[chunk + half : 2 * chunk] + high], axis=0)
    return near[2 * chunk :], send_x(after, 1), send_x(before, -1)


def step(
    teacher_hidden,
    teacher_head,
    student_hidden,
    student_head,
    pair_owner,
    pair_block,
    pair_shift,
    pair_count,
):
    tok_rows = student_hidden.shape[0]
    spots = jnp.stack([lax.axis_index("x"), lax.axis_index("c")]).astype(jnp.int32)

    rows = spread(teacher_hidden, "z", NZ)
    pieces = [student_head, send_x(student_head, -1), send_x(student_head, 1), send_x(student_head, 2)]
    head_mine = jnp.concatenate(pieces, axis=0)
    head_theirs = send_c(head_mine)
    rows = spread(rows, "y", NY)

    shift = by_source(pair_shift)
    place = by_source(pair_block * N_VOC + pair_owner).T.reshape(1, -1)
    count = by_source(pair_count).T.reshape(1, -1)
    head_full, student_logits, stats = kernel_call(
        student_kernel,
        (
            jax.ShapeDtypeStruct((DS, SCOLS), BF16),
            jax.ShapeDtypeStruct((tok_rows, SCOLS), F32),
            jax.ShapeDtypeStruct((tok_rows, BLOCK), F32),
        ),
        (),
        "svvv",
    )(spots, student_hidden, head_mine, head_theirs)
    rows, place, count, shift, stats = lax.optimization_barrier((rows, place, count, shift, stats))

    own, before, after = logit_parts(rows, teacher_head, spots)
    outgoing = kernel_call(
        softmax_kernel, jax.ShapeDtypeStruct((tok_rows, TCOLS + BLOCK), BF16), inputs="vvvv"
    )(own, before, after, stats)
    weight = kernel_call(
        weight_kernel, jax.ShapeDtypeStruct((SBLOCKS, FANOUT * TBLOCKS), BF16), inputs="vv"
    )(place, count)
    received = exchange(outgoing.reshape(N_VOC, OWN, TCOLS + BLOCK), ("z", "y"))
    received = received.transpose(1, 0, 2)
    rolled = kernel_call(
        roll_kernel, jax.ShapeDtypeStruct((FANOUT * TBLOCKS, OWN * BLOCK), BF16), inputs="vvv", flops=3_000_000_000
    )(received, base_kernel(), shift)
    target = kernel_call(
        align_kernel, jax.ShapeDtypeStruct((OWN, N_VOC, SCOLS + BLOCK), BF16), inputs="vvv"
    )(received, rolled, weight)
    target = exchange(target.transpose(1, 0, 2), ("z", "y")).reshape(tok_rows, SCOLS + BLOCK)

    turned = head_full.T
    lane_shape = jax.ShapeDtypeStruct((tok_rows, BLOCK), F32)
    grad, cross, log_total = kernel_call(
        grad_kernel,
        (jax.ShapeDtypeStruct((tok_rows, SCOLS), BF16), lane_shape, lane_shape),
        inputs="vv",
        flops=4_000_000_000,
    )(target, student_logits)
    terms = kernel_call(terms_kernel, jax.ShapeDtypeStruct((tok_rows, WIDE), F32), inputs="vvv")(grad, turned, cross)
    terms = exchange(terms.reshape(NY, tok_rows // NY, WIDE), "y").sum(axis=0)
    terms = exchange(terms.reshape(NZ, OWN, WIDE), "z")
    result = kernel_call(finish_kernel, jax.ShapeDtypeStruct((OWN, WIDE), BF16), inputs="v")(terms)
    result = spread(result, "z", NZ).reshape(NZ * OWN, WIDE)
    result = spread(result, "y", NY).reshape(tok_rows, WIDE)
    token_loss = log_total[:, 0] - unpack_lane(result[:, DS:], 0)[:, 0]
    return (token_loss, result[:, :DS])


def solution(mesh):
    grid = Mesh(mesh.devices.reshape(NX, NC, NZ, NY), ("x", "c", "z", "y"))
    tok = ("x", "c")
    voc = ("z", "y")
    in_specs = (
        P(voc, tok),
        P(tok, voc),
        P(tok, None),
        P(tok, voc),
        P(),
        P(),
        P(),
        P(),
    )
    out_specs = (P(tok), P(tok, None))
    return jax.shard_map(step, mesh=grid, in_specs=in_specs, out_specs=out_specs, check_vma=False)
```

```python
import jax
import jax.numpy as jnp
from jax import lax
from jax.experimental import pallas as pl
from jax.experimental.pallas import tpu as pltpu
from jax.sharding import Mesh
from jax.sharding import PartitionSpec as P


BLOCK = 128
TB_DEV = 8
SB_DEV = 10
FANOUT = 8
N_VOC = 64
NX, NC, NZ, NY = 4, 2, 16, 4
TBLOCKS = N_VOC * TB_DEV
SBLOCKS = N_VOC * SB_DEV
OWN = 2
DS = 1536
PIECE = DS // (NX * NC)
TCOLS = TB_DEV * BLOCK
SCOLS = SB_DEV * BLOCK
WIDE = DS + BLOCK

kernel_decay = 0.8
loss_scale = 256.0
F32 = jnp.float32
BF16 = jnp.bfloat16
VMEM_BYTES = 24 * 1024 * 1024


def kernel_call(kernel, out_shape, scratch=(), inputs="", flops=0):
    spaces = {"s": pltpu.SMEM, "v": pltpu.VMEM}
    return pl.pallas_call(
        kernel,
        out_shape=out_shape,
        in_specs=[pl.BlockSpec(memory_space=spaces[kind]) for kind in inputs],
        scratch_shapes=list(scratch),
        compiler_params=pltpu.CompilerParams(vmem_limit_bytes=VMEM_BYTES),
        cost_estimate=pl.CostEstimate(flops=flops, bytes_accessed=1 << 20, transcendentals=0) if flops else None,
    )


def base_kernel():
    row_index = lax.broadcasted_iota(jnp.int32, (BLOCK, BLOCK), 0)
    col_index = lax.broadcasted_iota(jnp.int32, (BLOCK, BLOCK), 1)
    distance = (row_index - col_index) % BLOCK
    distance = jnp.minimum(distance, BLOCK - distance)
    return jnp.power(F32(kernel_decay), distance.astype(F32)).astype(BF16)


def split_parts(value):
    first = value.astype(BF16).astype(F32)
    second = (value - first).astype(BF16).astype(F32)
    return first, second, value - first - second


def pack_lanes(rows, values):
    lanes = lax.broadcasted_iota(jnp.int32, (rows, BLOCK), 1)
    packed = jnp.zeros((rows, BLOCK), F32)
    for place, value in enumerate(values):
        for step, part in enumerate(split_parts(value)):
            packed = jnp.where(lanes == 3 * place + step, part, packed)
    return packed.astype(BF16)


def unpack_lane(packed, place):
    spot = 3 * place
    cols = packed[:, spot : spot + 3].astype(F32)
    return (cols[:, 0:1] + cols[:, 1:2]) + cols[:, 2:3]


def put_rows(full_ref, spots_ref, step, core, value):
    x = (spots_ref[0] + step) % NX
    start = (x * NC + core) * PIECE
    full_ref[pl.ds(pl.multiple_of(start, 64), PIECE), :] = value


def student_kernel(spots_ref, hidden_ref, mine_ref, theirs_ref, head_ref, logits_ref, stats_ref):
    c = spots_ref[1]
    for place, step in enumerate((0, 1, 3, 2)):
        rows = slice(place * PIECE, (place + 1) * PIECE)
        put_rows(head_ref, spots_ref, step, c, mine_ref[rows, :])
        put_rows(head_ref, spots_ref, step, 1 - c, theirs_ref[rows, :])
    logits = jnp.dot(hidden_ref[...], head_ref[...], preferred_element_type=F32)
    top = jnp.max(logits, axis=1, keepdims=True)
    total = jnp.sum(jnp.exp(logits - top), axis=1, keepdims=True)
    logits_ref[...] = logits
    lanes = lax.broadcasted_iota(jnp.int32, stats_ref.shape, 1)
    stats_ref[...] = jnp.where(lanes == 0, top, total)


def rows_kernel(spots_ref, gathered_ref, head_ref, far_ref, rest_ref, mine_ref, rows_ref, theirs_ref):
    x, c = spots_ref[0], spots_ref[1]
    part = gathered_ref.shape[0] // (NZ * NY)
    for spot in range(NY):
        for z in range(NZ):
            rows_ref[(z * NY + spot) * part : (z * NY + spot + 1) * part, :] = gathered_ref[
                (spot * NZ + z) * part : (spot * NZ + z + 1) * part, :
            ]
    chunk = far_ref.shape[0]
    for place, step in enumerate((2, 1, 3, 0)):
        first = ((x + step) % NX) * NC
        spot = slice(place * chunk, (place + 1) * chunk)
        theirs_ref[spot, :] = rows_ref[pl.ds(pl.multiple_of((first + 1 - c) * chunk, chunk), chunk), :]
        mine_ref[spot, :] = rows_ref[pl.ds(pl.multiple_of((first + c) * chunk, chunk), chunk), :]
    product = jnp.dot(theirs_ref[...], head_ref[...], preferred_element_type=F32)
    far_ref[...] = product[:chunk, :]
    rest_ref[...] = product[chunk:, :]


def softmax_kernel(own_ref, prev_ref, next_ref, stats_ref, out_ref):
    logits = own_ref[...] + prev_ref[...] + next_ref[...]
    peak = jnp.max(logits, axis=1, keepdims=True)
    out_ref[:, :TCOLS] = jnp.exp(logits - peak).astype(BF16)
    out_ref[:, TCOLS:] = pack_lanes(out_ref.shape[0], [peak, stats_ref[:, 0:1], stats_ref[:, 1:2]])


def weight_kernel(place_ref, count_ref, out_ref):
    place = place_ref[...]
    count = count_ref[...].astype(F32)
    for b in range(SB_DEV):
        rows = lax.broadcasted_iota(jnp.int32, (N_VOC, FANOUT * TBLOCKS), 0) + b * N_VOC
        out_ref[b * N_VOC : (b + 1) * N_VOC, :] = jnp.where(rows == place, count, 0.0).astype(BF16)


def roll_kernel(recv_ref, table_ref, shift_ref, rolled_ref):
    lanes = lax.broadcasted_iota(jnp.int32, (TBLOCKS, BLOCK), 1)
    for t in range(OWN):
        extra = recv_ref[t, :, TCOLS:]
        peak = unpack_lane(extra, 0)
        scale = jnp.exp(peak - jnp.max(peak, axis=0, keepdims=True))
        blocks = jnp.concatenate([recv_ref[t, :, j * BLOCK : (j + 1) * BLOCK] for j in range(TB_DEV)], axis=0)
        smooth = jnp.dot(blocks, table_ref[...], preferred_element_type=F32)
        smooth = (smooth * jnp.concatenate([scale] * TB_DEV, axis=0)).astype(BF16).astype(F32)
        for k in range(FANOUT):
            index = (lanes - shift_ref[:, k : k + 1]) & (BLOCK - 1)
            rolled = jnp.take_along_axis(smooth, index, axis=1)
            rolled_ref[k * TBLOCKS : (k + 1) * TBLOCKS, t * BLOCK : (t + 1) * BLOCK] = rolled.astype(BF16)


def align_kernel(recv_ref, rolled_ref, weight_ref, out_ref):
    aligned = jnp.dot(weight_ref[...], rolled_ref[...], preferred_element_type=F32)
    for t in range(OWN):
        mine = aligned[:, t * BLOCK : (t + 1) * BLOCK]
        norm = jnp.sum(jnp.sum(mine, axis=0, keepdims=True), axis=1, keepdims=True)
        mine = mine / norm
        for b in range(SB_DEV):
            out_ref[t, :, b * BLOCK : (b + 1) * BLOCK] = mine[b * N_VOC : (b + 1) * N_VOC, :].astype(BF16)
        extra = recv_ref[t, :, TCOLS:]
        top = unpack_lane(extra, 1)
        total = unpack_lane(extra, 2)
        joint_top = jnp.max(top, axis=0, keepdims=True)
        joint_total = jnp.sum(total * jnp.exp(top - joint_top), axis=0, keepdims=True)
        log_total = joint_top + jnp.log(joint_total)
        out_ref[t, :, SCOLS:] = pack_lanes(N_VOC, [log_total])


def grad_kernel(target_ref, logits_ref, grad_ref, cross_ref, log_ref):
    log_total = unpack_lane(target_ref[:, SCOLS:], 0)
    target = target_ref[:, :SCOLS].astype(F32)
    logits = logits_ref[...]
    cross = jnp.sum(target * logits, axis=1, keepdims=True)
    grad_ref[...] = (loss_scale * (jnp.exp(logits - log_total) - target)).astype(BF16)
    cross_ref[...] = jnp.broadcast_to(cross, cross_ref.shape)
    log_ref[...] = jnp.broadcast_to(log_total, log_ref.shape)


def terms_kernel(grad_ref, turned_ref, cross_ref, out_ref):
    out_ref[:, :DS] = jnp.dot(grad_ref[...], turned_ref[...], preferred_element_type=F32)
    out_ref[:, DS:] = cross_ref[...]


def finish_kernel(parts_ref, out_ref):
    terms = parts_ref[0]
    for i in range(1, NZ):
        terms = terms + parts_ref[i]
    out_ref[:, :DS] = terms[:, :DS].astype(BF16)
    out_ref[:, DS:] = pack_lanes(OWN, [terms[:, DS : DS + 1]])


def exchange(value, axis):
    return lax.all_to_all(value, axis, split_axis=0, concat_axis=0, tiled=True)


def spread(value, axis, size):
    return exchange(jnp.broadcast_to(value[None], (size,) + value.shape), axis)


def send(value, axis, size, step):
    return lax.ppermute(value, axis, [(i, (i + step) % size) for i in range(size)])


def send_x(value, step):
    return send(value, "x", NX, step)


def send_c(value):
    return lax.ppermute(value, "c", [(0, 1), (1, 0)])


def by_source(pairs):
    return pairs.reshape(N_VOC, TB_DEV, FANOUT).transpose(1, 0, 2).reshape(TBLOCKS, FANOUT)


def logit_parts(rows, head, spots):
    width = rows.shape[-1]
    rows = rows.reshape(-1, width)
    chunk = rows.shape[0] // (NX * NC)
    far_theirs, theirs, mine = kernel_call(
        rows_kernel,
        (
            jax.ShapeDtypeStruct((chunk, TCOLS), F32),
            jax.ShapeDtypeStruct((3 * chunk, TCOLS), F32),
            jax.ShapeDtypeStruct((4 * chunk, width), BF16),
        ),
        [pltpu.VMEM(rows.shape, BF16), pltpu.VMEM((4 * chunk, width), BF16)] ,
        "svv",
    )(spots, rows, head)
    far_theirs = send_c(far_theirs)
    theirs = send_c(theirs)
    mine = jnp.dot(mine, head, preferred_element_type=F32)
    far = mine[:chunk] + far_theirs
    half = chunk // 2
    low = send_x(far[:half], 1)
    high = send_x(far[half:], -1)
    near = mine[chunk:] + theirs
    after = jnp.concatenate([near[:half] + low, near[half:chunk]], axis=0)
    before = jnp.concatenate([near[chunk : chunk + half], near[chunk + half : 2 * chunk] + high], axis=0)
    return near[2 * chunk :], send_x(after, 1), send_x(before, -1)


def step(
    teacher_hidden,
    teacher_head,
    student_hidden,
    student_head,
    pair_owner,
    pair_block,
    pair_shift,
    pair_count,
):
    tok_rows = student_hidden.shape[0]
    spots = jnp.stack([lax.axis_index("x"), lax.axis_index("c")]).astype(jnp.int32)

    rows = spread(teacher_hidden, "z", NZ)
    pieces = [student_head, send_x(student_head, -1), send_x(student_head, 1), send_x(student_head, 2)]
    head_mine = jnp.concatenate(pieces, axis=0)
    head_theirs = send_c(head_mine)
    rows = spread(rows, "y", NY)

    shift = by_source(pair_shift)
    place = by_source(pair_block * N_VOC + pair_owner).T.reshape(1, -1)
    count = by_source(pair_count).T.reshape(1, -1)
    head_full, student_logits, stats = kernel_call(
        student_kernel,
        (
            jax.ShapeDtypeStruct((DS, SCOLS), BF16),
            jax.ShapeDtypeStruct((tok_rows, SCOLS), F32),
            jax.ShapeDtypeStruct((tok_rows, BLOCK), F32),
        ),
        (),
        "svvv",
    )(spots, student_hidden, head_mine, head_theirs)
    rows, place, count, shift, stats = lax.optimization_barrier((rows, place, count, shift, stats))

    own, before, after = logit_parts(rows, teacher_head, spots)
    outgoing = kernel_call(
        softmax_kernel, jax.ShapeDtypeStruct((tok_rows, TCOLS + BLOCK), BF16), inputs="vvvv"
    )(own, before, after, stats)
    weight = kernel_call(
        weight_kernel, jax.ShapeDtypeStruct((SBLOCKS, FANOUT * TBLOCKS), BF16), inputs="vv"
    )(place, count)
    received = exchange(outgoing.reshape(N_VOC, OWN, TCOLS + BLOCK), ("z", "y"))
    received, turned = lax.optimization_barrier((received, head_full.T))
    received = received.transpose(1, 0, 2)
    rolled = kernel_call(
        roll_kernel, jax.ShapeDtypeStruct((FANOUT * TBLOCKS, OWN * BLOCK), BF16), inputs="vvv", flops=3_000_000_000
    )(received, base_kernel(), shift)
    target = kernel_call(
        align_kernel, jax.ShapeDtypeStruct((OWN, N_VOC, SCOLS + BLOCK), BF16), inputs="vvv"
    )(received, rolled, weight)
    target = exchange(target.transpose(1, 0, 2), ("z", "y")).reshape(tok_rows, SCOLS + BLOCK)

    lane_shape = jax.ShapeDtypeStruct((tok_rows, BLOCK), F32)
    grad, cross, log_total = kernel_call(
        grad_kernel,
        (jax.ShapeDtypeStruct((tok_rows, SCOLS), BF16), lane_shape, lane_shape),
        inputs="vv",
        flops=4_000_000_000,
    )(target, student_logits)
    terms = kernel_call(terms_kernel, jax.ShapeDtypeStruct((tok_rows, WIDE), F32), inputs="vvv")(grad, turned, cross)
    terms = exchange(terms.reshape(NY, tok_rows // NY, WIDE), "y").sum(axis=0)
    terms = exchange(terms.reshape(NZ, OWN, WIDE), "z")
    result = kernel_call(finish_kernel, jax.ShapeDtypeStruct((OWN, WIDE), BF16), inputs="v")(terms)
    result = spread(result, "z", NZ).reshape(NZ * OWN, WIDE)
    result = spread(result, "y", NY).reshape(tok_rows, WIDE)
    token_loss = log_total[:, 0] - unpack_lane(result[:, DS:], 0)[:, 0]
    return (token_loss, result[:, :DS])


def solution(mesh):
    grid = Mesh(mesh.devices.reshape(NX, NC, NZ, NY), ("x", "c", "z", "y"))
    tok = ("x", "c")
    voc = ("z", "y")
    in_specs = (
        P(voc, tok),
        P(tok, voc),
        P(tok, None),
        P(tok, voc),
        P(),
        P(),
        P(),
        P(),
    )
    out_specs = (P(tok), P(tok, None))
    return jax.shard_map(step, mesh=grid, in_specs=in_specs, out_specs=out_specs, check_vma=False)
```
